256 devices in a mesh: row: 16 (over z_hi, x, core), grp: 16 (over y, z_lo).
Axes of the slice: x: 4, y: 4, z: 8 (z_hi: 2, z_lo: 4; z = z_hi * 4 + z_lo), core: 2. Of those that a mesh axis runs over, the one named last changes fastest.
Arguments:
- view_x: bfloat16 [65536, 1024], P(('row', 'grp')), may hold values from -64 to 64
- view_y: bfloat16 [65536, 1024], P(('row', 'grp')), may hold values from -64 to 64
Outputs:
- coherence: float32 [1024, 1024], P(('row', 'grp'))
The draws below stay inside these ranges and needn't reach their ends.
All inputs are finite; a program needn't handle non-finite values.
Results may differ from the reference program's by a relative error of at most 0.0003.
Values sent between devices are 32-bit elements; how exact they have to be, the bound alone decides.
No kernel may reach another device: no remote copies, remote signals or barrier semaphores. Data moves between devices by JAX's collectives and lax.ppermute only.
A program may use at most 128 MiB of HBM per device.

```python
import math
import jax
import jax.numpy as jnp
from jax import lax

D = 1024
TOK_DEV = 256
TOKENS = 65536


def shared_views(key):
    key_base = jax.random.fold_in(key, 101)
    key_nx = jax.random.fold_in(key, 102)
    key_ny = jax.random.fold_in(key, 103)
    key_rx = jax.random.fold_in(key, 104)
    key_ry = jax.random.fold_in(key, 105)
    base = jax.random.normal(key_base, (TOKENS, D), jnp.float32)
    positions = jnp.arange(TOKENS, dtype=jnp.int32)
    block = positions // TOK_DEV
    blocks = TOKENS // TOK_DEV
    columns = jnp.arange(D, dtype=jnp.int32)
    offset = (1 + 7 * block) % D
    index = (columns[None, :] + offset[:, None]) % D
    moved = jnp.take_along_axis(base, index, axis=1)
    near = jnp.roll(base, 1, axis=1)
    trend = jnp.exp(math.log(3.0) * block.astype(jnp.float32) / max(blocks - 1, 1))
    noise_x = jax.random.normal(key_nx, (TOKENS, D), jnp.float32)
    noise_y = jax.random.normal(key_ny, (TOKENS, D), jnp.float32)
    row_x = jnp.exp(jax.random.uniform(key_rx, (TOKENS, 1), jnp.float32, 0.0, math.log(2.0)))
    row_y = jnp.exp(jax.random.uniform(key_ry, (TOKENS, 1), jnp.float32, 0.0, math.log(2.0)))
    first = (base + 0.5 * noise_x) * row_x * trend[:, None]
    second = (0.6 * base + 0.8 * near + moved + 0.5 * noise_y) * row_y * trend[:, None]
    return (jnp.clip(first, -64.0, 64.0), jnp.clip(second, -64.0, 64.0))


def draw_view_x(key, part):
    return shared_views(key)[0].astype(jnp.bfloat16)


def draw_view_y(key, part):
    return shared_views(key)[1].astype(jnp.bfloat16)


def setup_inputs(seed: int = 0) -> dict:
    splits = jax.random.split(jax.random.key(seed), 3)
    view_x = draw_view_x(jax.random.fold_in(splits[2], 71), 0)
    view_y = draw_view_y(jax.random.fold_in(splits[2], 71), 0)
    return {"view_x": view_x, "view_y": view_y}


def gram_of(left, right):
    return lax.dot_general(left.astype(jnp.float32), right.astype(jnp.float32), (((0,), (0,)), ((), ())), preferred_element_type=jnp.float32)

def reference(view_x, view_y):
    gram_x = gram_of(view_x, view_x)
    gram_y = gram_of(view_y, view_y)
    cross = gram_of(view_x, view_y)
    lower_x = jnp.linalg.cholesky(gram_x)
    lower_y = jnp.linalg.cholesky(gram_y)
    whiten = jax.scipy.linalg.solve_triangular(lower_y, cross.T, lower=True).T
    return jax.scipy.linalg.solve_triangular(lower_x, whiten, lower=True)
```

```python
import functools

import jax
import jax.numpy as jnp
from jax import lax
from jax.experimental import pallas as pl
from jax.experimental.pallas import tpu as pltpu
from jax.sharding import Mesh
from jax.sharding import PartitionSpec as P

AXES = ("z_hi", "x", "core", "y", "z_lo")
SIZES = (2, 4, 2, 4, 4)
PLANE = ("x", "y")
LINE = ("z_hi", "z_lo")
N, NB, SB, G = 1024, 128, 32, 8
KB = N // NB
OWNED = 4
UPPER = [(i, j) for i in range(KB) for j in range(i, KB)]
EARLY, LATE = UPPER[:16], UPPER[16:]
LATE_SLOTS = 24
VMEM = pl.BlockSpec(memory_space=pltpu.VMEM)
SMEM = pl.BlockSpec(memory_space=pltpu.SMEM)


def mm(a, b, dims):
    return lax.dot_general(
        a, b, (dims, ((), ())), precision=lax.Precision.HIGHEST, preferred_element_type=jnp.float32
    )


def call(kernel, outs, n_smem, n_vmem, scratch=(), flops=0, bytes_accessed=0):
    return pl.pallas_call(
        kernel,
        out_shape=[jax.ShapeDtypeStruct(s, jnp.float32) for s in outs],
        in_specs=[SMEM] * n_smem + [VMEM] * n_vmem,
        out_specs=[VMEM] * len(outs),
        scratch_shapes=list(scratch),
        compiler_params=pltpu.CompilerParams(vmem_limit_bytes=40 << 20),
        cost_estimate=pl.CostEstimate(flops=flops, bytes_accessed=bytes_accessed, transcendentals=0),
    )


def gram_kernel(blocks, slots, core, x, y, mine, other, pick):
    for out, which in ((mine, 0), (other, 1)):
        @pl.when(core[0] == which)
        def _():
            pick[...] = x[...]

        @pl.when(core[0] != which)
        def _():
            pick[...] = y[...]

        for i in sorted({i for i, _ in blocks}):
            cols = [j for a, j in blocks if a == i]
            lo, hi = min(cols), max(cols) + 1
            prod = lax.dot_general(
                pick[:, i * NB:(i + 1) * NB], pick[:, lo * NB:hi * NB], (((0,), (0,)), ((), ())),
                preferred_element_type=jnp.float32,
            )
            for j in cols:
                at = blocks.index((i, j))
                out[at * NB:(at + 1) * NB, :] = prod[:, (j - lo) * NB:(j - lo + 1) * NB]
        if slots > len(blocks):
            out[len(blocks) * NB:, :] = jnp.zeros(((slots - len(blocks)) * NB, NB), jnp.float32)


def cross_kernel(core, x, y, mine, other):
    half = N // 2
    for out, which in ((mine, core[0]), (other, 1 - core[0])):
        left = x[:, pl.ds(pl.multiple_of(which * half, half), half)]
        for j in range(KB // 2):
            prod = lax.dot_general(
                left, y[:, 2 * j * NB:2 * (j + 1) * NB], (((0,), (0,)), ((), ())), preferred_element_type=jnp.float32
            )
            for i in range(half // NB):
                for d in range(2):
                    at = i * KB + 2 * j + d
                    out[at * NB:(at + 1) * NB, :] = prod[i * NB:(i + 1) * NB, d * NB:(d + 1) * NB]


def exchange(pieces, axes):
    return lax.all_to_all(pieces, axes, 0, 0, tiled=True)


def spread(piece, n):
    return jnp.broadcast_to(piece[None], (n, *piece.shape))


def sum_of_chips(mine, other, name):
    with jax.named_scope(name):
        rows = mine.shape[0]
        total = mine + lax.ppermute(other, "core", [(0, 1), (1, 0)])
        piece = jnp.sum(exchange(total.reshape(16, rows // 16, NB), PLANE), axis=0)
        part = jnp.sum(exchange(piece.reshape(8, rows // 128, NB), LINE), axis=0)
        piece = exchange(spread(part, 8), LINE).reshape(rows // 16, NB)
        return exchange(spread(piece, 16), PLANE).reshape(rows, NB)


def tile(v):
    return jnp.broadcast_to(v, (G, NB))


def pivots(s):
    l = [[None] * G for _ in range(G)]
    r = [None] * G
    for k in range(G):
        r[k] = lax.rsqrt(s[k][k])
        for j in range(k + 1, G):
            l[j][k] = s[k][j] * r[k]
        for i in range(k + 1, G):
            for j in range(i, G):
                s[i][j] = s[i][j] - l[i][k] * l[j][k]
    return l, r


def forward(l, r, rows):
    out = []
    for k in range(G):
        v = rows[k]
        for j in range(k):
            v = v - l[k][j] * out[j]
        out.append(v * r[k])
    return out


def factor_block(work):
    groups = SB // G
    for top in range(0, NB, SB):
        left = [work[top + G * g:top + G * (g + 1), :NB] for g in range(groups)]
        right = [work[top + G * g:top + G * (g + 1), NB:] for g in range(groups)]
        for p in range(groups):
            c0 = top + G * p
            s = [[tile(left[p][i:i + 1, c0 + j:c0 + j + 1]) if j >= i else None for j in range(G)] for i in range(G)]
            cols = [
                [jnp.broadcast_to(left[q][:, c0 + k:c0 + k + 1], (G, NB)) for k in range(G)]
                for q in range(p + 1, groups)
            ]
            l, r = pivots(s)
            u = forward(l, r, [tile(left[p][i:i + 1, :]) for i in range(G)])
            b = forward(l, r, [tile(right[p][i:i + 1, :]) for i in range(G)])
            for i in range(G):
                work[c0 + i:c0 + i + 1, :NB] = u[i][0:1]
                work[c0 + i:c0 + i + 1, NB:] = b[i][0:1]
            for q in range(p + 1, groups):
                lc = forward(l, r, cols[q - p - 1])
                for k in range(G):
                    left[q] = left[q] - lc[k] * u[k]
                    right[q] = right[q] - lc[k] * b[k]
        rest = top + SB
        if rest < NB:
            rows = work[top:rest, :]
            work[rest:, :] -= mm(rows[:, rest:NB], rows, ((0,), (0,)))


def eliminate(first, last, upto, upper, inverse, work):
    eye = lax.broadcasted_iota(jnp.int32, (NB, NB), 0) == lax.broadcasted_iota(jnp.int32, (NB, NB), 1)

    def step(k, carry):
        at = pl.multiple_of(k * NB, NB)
        work[:, :NB] = upper[pl.ds(at, NB), pl.ds(at, NB)]
        work[:, NB:] = eye.astype(jnp.float32)
        factor_block(work)
        inverse[pl.ds(at, NB), :] = work[:, NB:]
        for kk in range(first, min(last, KB - 1)):
            @pl.when(k == kk)
            def _():
                lo, nxt = kk * NB, (kk + 1) * NB
                upper[lo:nxt, nxt:] = mm(work[:, NB:], upper[lo:nxt, nxt:], ((1,), (0,)))
                for i in range(kk + 1, upto):
                    rows = upper[lo:nxt, i * NB:]
                    upper[i * NB:(i + 1) * NB, i * NB:] -= mm(rows[:, :NB], rows, ((0,), (0,)))
        return carry

    lax.fori_loop(first, last, step, 0)


def early_kernel(blocks, upper, inverse, work):
    for at, (i, j) in enumerate(EARLY[:15]):
        upper[i * NB:(i + 1) * NB, j * NB:(j + 1) * NB] = blocks[at * NB:(at + 1) * NB, :]
    eliminate(0, 2, 2, upper, inverse, work)


def late_kernel(rows, early, late, top, top_inverse, upper, inverse, z, work):
    upper[:2 * NB, :] = top[...]
    inverse[:2 * NB, :] = top_inverse[...]
    upper[2 * NB:3 * NB, 2 * NB:3 * NB] = early[15 * NB:16 * NB, :]
    for at, (i, j) in enumerate(LATE):
        upper[i * NB:(i + 1) * NB, j * NB:(j + 1) * NB] = late[at * NB:(at + 1) * NB, :]
    for i in range(2, KB):
        both = upper[:2 * NB, i * NB:]
        upper[i * NB:(i + 1) * NB, i * NB:] -= mm(both[:, :NB], both, ((0,), (0,)))
    eliminate(2, KB, KB, upper, inverse, work)
    line = lax.broadcasted_iota(jnp.int32, (G, NB), 0)
    want = jnp.where(line < OWNED, rows[0] + line, rows[1] + line - OWNED)
    lane = lax.broadcasted_iota(jnp.int32, (G, NB), 1)
    for k in reversed(range(KB)):
        v = (want == lane + k * NB).astype(jnp.float32)
        if k < KB - 1:
            v = v - mm(z[:, (k + 1) * NB:], upper[k * NB:(k + 1) * NB, (k + 1) * NB:], ((1,), (1,)))
        z[:, k * NB:(k + 1) * NB] = mm(v, inverse[k * NB:(k + 1) * NB, :], ((1,), (0,)))


def apply_kernel(core, z_own, z_sent, cross, out):
    half = N // 2
    z = jnp.where(core[0] == 0, z_own[:, :half], z_sent[:, half:])
    acc = jnp.zeros((G, N), jnp.float32)
    for i in range(half // NB):
        row = jnp.concatenate([cross[(i * KB + j) * NB:(i * KB + j + 1) * NB, :] for j in range(KB)], axis=1)
        acc = acc + mm(z[:, i * NB:(i + 1) * NB], row, ((1,), (0,)))
    out[...] = acc


def solve_kernel(w_own, w_sent, upper, inverse, y):
    w = w_own[...] + w_sent[...]
    for k in range(KB):
        v = w[:, k * NB:(k + 1) * NB]
        if k:
            v = v - mm(y[:, :k * NB], upper[:k * NB, k * NB:(k + 1) * NB], ((1,), (0,)))
        y[:, k * NB:(k + 1) * NB] = mm(v, inverse[k * NB:(k + 1) * NB, :], ((1,), (1,)))


def on_device(view_x, view_y):
    core = lax.axis_index("core")
    core_ref = core.astype(jnp.int32).reshape(1)
    chip = ((lax.axis_index("z_hi") * 4 + lax.axis_index("x")) * 2) * 16 + lax.axis_index("y") * 4 + lax.axis_index("z_lo")
    rows = jnp.stack([chip * OWNED, (chip + 16) * OWNED]).astype(jnp.int32)
    work = pltpu.VMEM((NB, 2 * NB), jnp.float32)
    pick = pltpu.VMEM(view_x.shape, view_x.dtype)

    sums = []
    for blocks, slots, name in ((EARLY, 16, "early"), (LATE, LATE_SLOTS, "late")):
        mine, other = call(
            functools.partial(gram_kernel, blocks, slots), [(slots * NB, NB)] * 2, 1, 2, [pick], flops=10**9
        )(core_ref, view_x, view_y)
        sums.append(sum_of_chips(mine, other, name))
    early, late = sums
    mine, other = call(cross_kernel, [(32 * NB, NB)] * 2, 1, 2, flops=10**9)(core_ref, view_x, view_y)
    cross = sum_of_chips(mine, other, "cross")

    top, top_inverse = call(early_kernel, [(2 * NB, N), (2 * NB, NB)], 0, 1, [work], flops=10**10)(early)
    upper, inverse, z = call(late_kernel, [(N, N), (N, NB), (G, N)], 1, 4, [work], flops=3 * 10**10)(
        rows, early, late, top, top_inverse
    )
    z_sent = lax.ppermute(z, "core", [(0, 1), (1, 0)])
    (w,) = call(apply_kernel, [(G, N)], 1, 3)(core_ref, z, z_sent, cross)
    w_sent = lax.ppermute(w, "core", [(0, 1), (1, 0)])
    (y,) = call(solve_kernel, [(G, N)], 0, 4)(w, w_sent, upper, inverse)
    y_sent = lax.ppermute(y[:OWNED], "core", [(0, 1), (1, 0)])
    return jnp.where(core == 0, y_sent, y[OWNED:])


def solution(mesh):
    fine = Mesh(mesh.devices.reshape(SIZES), AXES)
    spec = P(AXES, None)
    return jax.shard_map(on_device, mesh=fine, in_specs=(spec, spec), out_specs=spec, check_vma=False)
```

```python
import functools

import jax
import jax.numpy as jnp
from jax import lax
from jax.experimental import pallas as pl
from jax.experimental.pallas import tpu as pltpu
from jax.sharding import Mesh
from jax.sharding import PartitionSpec as P

AXES = ("z_hi", "x", "core", "y", "z_lo")
SIZES = (2, 4, 2, 4, 4)
PLANE = ("x", "y")
LINE = ("z_hi", "z_lo")
N, NB, SB, G = 1024, 128, 32, 8
KB = N // NB
OWNED = 4
HEAD = 4
EARLY = [(i, j) for i in range(HEAD) for j in range(i, HEAD)]
LATE = [(i, j) for i in range(KB) for j in range(max(i, HEAD), KB)]
LATE_SLOTS = 40 - len(EARLY)
STEP = 16
VMEM = pl.BlockSpec(memory_space=pltpu.VMEM)
SMEM = pl.BlockSpec(memory_space=pltpu.SMEM)


def mm(a, b, dims):
    return lax.dot_general(
        a, b, (dims, ((), ())), precision=lax.Precision.HIGHEST, preferred_element_type=jnp.float32
    )


def call(kernel, outs, n_smem, n_vmem, scratch=(), flops=0, bytes_accessed=0):
    return pl.pallas_call(
        kernel,
        out_shape=[jax.ShapeDtypeStruct(s, jnp.float32) for s in outs],
        in_specs=[SMEM] * n_smem + [VMEM] * n_vmem,
        out_specs=[VMEM] * len(outs),
        scratch_shapes=list(scratch),
        compiler_params=pltpu.CompilerParams(vmem_limit_bytes=16 << 20),
        cost_estimate=pl.CostEstimate(flops=flops, bytes_accessed=bytes_accessed, transcendentals=0),
    )


def gram_kernel(core, x, y, mine, other, pick):
    early_rows, late_rows = len(EARLY) * NB // 16, LATE_SLOTS * NB // 16
    for out, which in ((mine, 0), (other, 1)):
        @pl.when(core[0] == which)
        def _():
            pick[...] = x[...]

        @pl.when(core[0] != which)
        def _():
            pick[...] = y[...]

        for i in range(KB):
            prod = lax.dot_general(
                pick[:, i * NB:(i + 1) * NB], pick[:, i * NB:], (((0,), (0,)), ((), ())),
                preferred_element_type=jnp.float32,
            )
            for j in range(i, KB):
                early = (i, j) in EARLY
                at = (EARLY if early else LATE).index((i, j)) * NB
                rows, base = (early_rows, 0) if early else (late_rows, early_rows)
                for t in range(0, NB, STEP):
                    part, line = divmod(at + t, rows)
                    out[part, base + line:base + line + STEP, :] = prod[t:t + STEP, (j - i) * NB:(j - i + 1) * NB]
        for at in range(len(LATE) * NB, LATE_SLOTS * NB, STEP):
            part, line = divmod(at, late_rows)
            out[part, early_rows + line:early_rows + line + STEP, :] = jnp.zeros((STEP, NB), jnp.float32)


def cross_kernel(core, x, y, mine, other):
    half = N // 2
    for out, which in ((mine, core[0]), (other, 1 - core[0])):
        left = x[:, pl.ds(pl.multiple_of(which * half, half), half)]
        for j in range(KB // 2):
            prod = lax.dot_general(
                left, y[:, 2 * j * NB:2 * (j + 1) * NB], (((0,), (0,)), ((), ())), preferred_element_type=jnp.float32
            )
            for i in range(half // NB):
                for d in range(2):
                    at = i * KB + 2 * j + d
                    out[at * NB:(at + 1) * NB, :] = prod[i * NB:(i + 1) * NB, d * NB:(d + 1) * NB]


def exchange(pieces, axes):
    return lax.all_to_all(pieces, axes, 0, 0, tiled=True)


def spread(piece, n):
    return jnp.broadcast_to(piece[None], (n, *piece.shape))


def swap(a):
    return lax.ppermute(a, "core", [(0, 1), (1, 0)])


def tile(v):
    return jnp.broadcast_to(v, (G, NB))


def pivots(s):
    l = [[None] * G for _ in range(G)]
    r = [None] * G
    for k in range(G):
        r[k] = lax.rsqrt(s[k][k])
        for j in range(k + 1, G):
            l[j][k] = s[k][j] * r[k]
        for i in range(k + 1, G):
            for j in range(i, G):
                s[i][j] = s[i][j] - l[i][k] * l[j][k]
    return l, r


def forward(l, r, rows):
    out = []
    for k in range(G):
        v = rows[k]
        for j in range(k):
            v = v - l[k][j] * out[j]
        out.append(v * r[k])
    return out


def factor_block(work):
    groups = SB // G
    for top in range(0, NB, SB):
        left = [work[top + G * g:top + G * (g + 1), :NB] for g in range(groups)]
        right = [work[top + G * g:top + G * (g + 1), NB:] for g in range(groups)]
        for p in range(groups):
            c0 = top + G * p
            s = [[tile(left[p][i:i + 1, c0 + j:c0 + j + 1]) if j >= i else None for j in range(G)] for i in range(G)]
            cols = [
                [jnp.broadcast_to(left[q][:, c0 + k:c0 + k + 1], (G, NB)) for k in range(G)]
                for q in range(p + 1, groups)
            ]
            l, r = pivots(s)
            u = forward(l, r, [tile(left[p][i:i + 1, :]) for i in range(G)])
            b = forward(l, r, [tile(right[p][i:i + 1, :]) for i in range(G)])
            for i in range(G):
                work[c0 + i:c0 + i + 1, :NB] = u[i][0:1]
                work[c0 + i:c0 + i + 1, NB:] = b[i][0:1]
            for q in range(p + 1, groups):
                lc = forward(l, r, cols[q - p - 1])
                for k in range(G):
                    left[q] = left[q] - lc[k] * u[k]
                    right[q] = right[q] - lc[k] * b[k]
        rest = top + SB
        if rest < NB:
            rows = work[top:rest, :]
            work[rest:, :] -= mm(rows[:, rest:NB], rows, ((0,), (0,)))


def eliminate(first, last, width, upper, inverse, work):
    eye = lax.broadcasted_iota(jnp.int32, (NB, NB), 0) == lax.broadcasted_iota(jnp.int32, (NB, NB), 1)

    def step(k, carry):
        at = pl.multiple_of(k * NB, NB)
        work[:, :NB] = upper[pl.ds(at, NB), pl.ds(at, NB)]
        work[:, NB:] = eye.astype(jnp.float32)
        factor_block(work)
        inverse[pl.ds(at, NB), :] = work[:, NB:]
        for kk in range(first, min(last, width - 1)):
            @pl.when(k == kk)
            def _():
                lo, nxt, end = kk * NB, (kk + 1) * NB, width * NB
                upper[lo:nxt, nxt:end] = mm(work[:, NB:], upper[lo:nxt, nxt:end], ((1,), (0,)))
                for i in range(kk + 1, width):
                    rows = upper[lo:nxt, i * NB:end]
                    upper[i * NB:(i + 1) * NB, i * NB:end] -= mm(rows[:, :NB], rows, ((0,), (0,)))
        return carry

    lax.fori_loop(first, last, step, 0)


def head_kernel(blocks, upper, inverse, work):
    for at, (i, j) in enumerate(EARLY):
        upper[i * NB:(i + 1) * NB, j * NB:(j + 1) * NB] = blocks[at * NB:(at + 1) * NB, :]
    eliminate(0, HEAD, HEAD, upper, inverse, work)


def middle_kernel(last, blocks, head, head_inverse, upper, inverse, work):
    h = HEAD * NB
    upper[:h, :h] = head[...]
    inverse[:h, :] = head_inverse[...]
    for at, (i, j) in enumerate(LATE):
        upper[i * NB:(i + 1) * NB, j * NB:(j + 1) * NB] = blocks[at * NB:(at + 1) * NB, :]
    for k in range(HEAD):
        lo, nxt = k * NB, (k + 1) * NB
        v = upper[lo:nxt, h:]
        if k:
            v = v - mm(upper[:lo, lo:nxt], upper[:lo, h:], ((0,), (0,)))
        upper[lo:nxt, h:] = mm(inverse[lo:nxt, :], v, ((1,), (0,)))
    for i in range(HEAD, KB):
        done = upper[:h, i * NB:]
        upper[i * NB:(i + 1) * NB, i * NB:] -= mm(done[:, :NB], done, ((0,), (0,)))
    eliminate(HEAD, last, KB, upper, inverse, work)


def tail_kernel(first, rows, upper_in, inverse_in, upper, inverse, z, work):
    eliminate(first, KB, KB, upper, inverse, work)
    line = lax.broadcasted_iota(jnp.int32, (G, NB), 0)
    want = jnp.where(line < OWNED, rows[0] + line, rows[1] + line - OWNED)
    lane = lax.broadcasted_iota(jnp.int32, (G, NB), 1)
    for k in reversed(range(KB)):
        v = (want == lane + k * NB).astype(jnp.float32)
        if k < KB - 1:
            v = v - mm(z[:, (k + 1) * NB:], upper[k * NB:(k + 1) * NB, (k + 1) * NB:], ((1,), (1,)))
        z[:, k * NB:(k + 1) * NB] = mm(v, inverse[k * NB:(k + 1) * NB, :], ((1,), (0,)))


def apply_kernel(core, z_own, z_sent, cross, out):
    half = N // 2
    z = jnp.where(core[0] == 0, z_own[:, :half], z_sent[:, half:])
    acc = jnp.zeros((G, N), jnp.float32)
    for i in range(half // NB):
        row = jnp.concatenate([cross[(i * KB + j) * NB:(i * KB + j + 1) * NB, :] for j in range(KB)], axis=1)
        acc = acc + mm(z[:, i * NB:(i + 1) * NB], row, ((1,), (0,)))
    out[...] = acc


def solve_kernel(w_own, w_sent, upper, inverse, y):
    w = w_own[...] + w_sent[...]
    for k in range(KB):
        v = w[:, k * NB:(k + 1) * NB]
        if k:
            v = v - mm(y[:, :k * NB], upper[:k * NB, k * NB:(k + 1) * NB], ((1,), (0,)))
        y[:, k * NB:(k + 1) * NB] = mm(v, inverse[k * NB:(k + 1) * NB, :], ((1,), (1,)))


def after(value, *others):
    return lax.optimization_barrier((value, *others))[0]


def on_device(view_x, view_y):
    core = lax.axis_index("core")
    core_ref = core.astype(jnp.int32).reshape(1)
    chip = ((lax.axis_index("z_hi") * 4 + lax.axis_index("x")) * 2) * 16 + lax.axis_index("y") * 4 + lax.axis_index("z_lo")
    rows = jnp.stack([chip * OWNED, (chip + 16) * OWNED]).astype(jnp.int32)
    work = pltpu.VMEM((NB, 2 * NB), jnp.float32)
    early_rows, late_rows = len(EARLY) * NB // 16, LATE_SLOTS * NB // 16
    part = early_rows + late_rows

    with jax.named_scope("gram"):
        mine, other = call(
            gram_kernel, [(16, part, NB)] * 2, 1, 2, [pltpu.VMEM(view_x.shape, view_x.dtype)], flops=2 * 10**9
        )(core_ref, view_x, view_y)
        gram = mine + swap(other)
    with jax.named_scope("cross"):
        keep, give = call(cross_kernel, [(32 * NB, NB)] * 2, 1, 2, flops=10**9)(
            core_ref, *after((view_x, view_y), mine)
        )
        cross = keep + swap(give)
        for axis in PLANE:
            cross = lax.psum_scatter(cross, axis, scatter_dimension=0, tiled=True)
    with jax.named_scope("gram"):
        piece = jnp.sum(exchange(gram, PLANE), axis=0)
        share = jnp.sum(exchange(piece.reshape(8, part // 8, NB), LINE), axis=0)
    with jax.named_scope("both"):
        both = exchange(jnp.concatenate([spread(share, 8), cross.reshape(8, -1, NB)], axis=1), LINE)
        piece = both[:, :part // 8].reshape(part, NB)
        early = exchange(spread(piece[:early_rows], 16), PLANE).reshape(16 * early_rows, NB)
        both = after(both, early)
        piece = both[:, :part // 8].reshape(part, NB)
        late = exchange(spread(piece[early_rows:], 16), PLANE).reshape(16 * late_rows, NB)
        cross = jnp.sum(both[:, part // 8:], axis=0)

    head, head_inverse = call(
        head_kernel, [(HEAD * NB, HEAD * NB), (HEAD * NB, NB)], 0, 1, [work], flops=3 * 10**10
    )(early)
    with jax.named_scope("cross_back"):
        cross = after(cross, head)
        cross = exchange(spread(cross, 8), LINE).reshape(256, NB)
    upper, inverse = call(
        functools.partial(middle_kernel, 5), [(N, N), (N, NB)], 0, 3, [work], flops=10**10
    )(late, head, head_inverse)
    with jax.named_scope("cross_back"):
        cross = exchange(spread(after(cross, upper), 16), PLANE).reshape(32 * NB, NB)
    upper, inverse, z = pl.pallas_call(
        functools.partial(tail_kernel, 5),
        out_shape=[jax.ShapeDtypeStruct(s, jnp.float32) for s in ((N, N), (N, NB), (G, N))],
        in_specs=[SMEM, VMEM, VMEM],
        out_specs=[VMEM] * 3,
        scratch_shapes=[work],
        input_output_aliases={1: 0, 2: 1},
        compiler_params=pltpu.CompilerParams(vmem_limit_bytes=16 << 20),
        cost_estimate=pl.CostEstimate(flops=3 * 10**10, bytes_accessed=0, transcendentals=0),
    )(rows, upper, inverse)
    (w,) = call(apply_kernel, [(G, N)], 1, 3)(core_ref, z, swap(z), cross)
    (y,) = call(solve_kernel, [(G, N)], 0, 4)(w, swap(w), upper, inverse)
    y_sent = swap(y[:OWNED])
    return jnp.where(core == 0, y_sent, y[OWNED:])


def solution(mesh):
    fine = Mesh(mesh.devices.reshape(SIZES), AXES)
    spec = P(AXES, None)
    return jax.shard_map(on_device, mesh=fine, in_specs=(spec, spec), out_specs=spec, check_vma=False)
```

```python
import functools

import jax
import jax.numpy as jnp
from jax import lax
from jax.experimental import pallas as pl
from jax.experimental.pallas import tpu as pltpu
from jax.sharding import Mesh
from jax.sharding import PartitionSpec as P

AXES = ("z_hi", "x", "core", "y", "z_lo")
SIZES = (2, 4, 2, 4, 4)
PLANE = ("x", "y")
LINE = ("z_hi", "z_lo")
N, NB, SB, G = 1024, 128, 32, 8
KB = N // NB
OWNED = 4
HEAD = 5
EARLY = [(i, j) for i in range(HEAD) for j in range(i, HEAD)]
LATE = [(i, j) for i in range(KB) for j in range(max(i, HEAD), KB)]
LATE_SLOTS = 40 - len(EARLY)
STEP = 8
EARLY_ROWS = len(EARLY) * NB // 16
GRAM = 40 * NB // 16
PART = GRAM + N // 2 * N // NB // 16
VMEM = pl.BlockSpec(memory_space=pltpu.VMEM)
SMEM = pl.BlockSpec(memory_space=pltpu.SMEM)


def mm(a, b, dims):
    return lax.dot_general(
        a, b, (dims, ((), ())), precision=lax.Precision.HIGHEST, preferred_element_type=jnp.float32
    )


def call(kernel, outs, n_smem, n_vmem, scratch=(), flops=0, bytes_accessed=0):
    return pl.pallas_call(
        kernel,
        out_shape=[jax.ShapeDtypeStruct(s, jnp.float32) for s in outs],
        in_specs=[SMEM] * n_smem + [VMEM] * n_vmem,
        out_specs=[VMEM] * len(outs),
        scratch_shapes=list(scratch),
        compiler_params=pltpu.CompilerParams(vmem_limit_bytes=16 << 20),
        cost_estimate=pl.CostEstimate(flops=flops, bytes_accessed=bytes_accessed, transcendentals=0),
    )


def gram_kernel(core, x, y, mine, other, pick):
    early_rows, late_rows = EARLY_ROWS, GRAM - EARLY_ROWS
    for out, which in ((mine, 0), (other, 1)):
        @pl.when(core[0] == which)
        def _():
            pick[...] = x[...]

        @pl.when(core[0] != which)
        def _():
            pick[...] = y[...]

        for i in range(KB):
            prod = lax.dot_general(
                pick[:, i * NB:(i + 1) * NB], pick[:, i * NB:], (((0,), (0,)), ((), ())),
                preferred_element_type=jnp.float32,
            )
            for j in range(i, KB):
                early = (i, j) in EARLY
                at = (EARLY if early else LATE).index((i, j)) * NB
                rows, base = (early_rows, 0) if early else (late_rows, early_rows)
                for t in range(0, NB, STEP):
                    part, line = divmod(at + t, rows)
                    out[part, base + line:base + line + STEP, :] = prod[t:t + STEP, (j - i) * NB:(j - i + 1) * NB]
        for at in range(len(LATE) * NB, LATE_SLOTS * NB, STEP):
            part, line = divmod(at, late_rows)
            out[part, early_rows + line:early_rows + line + STEP, :] = jnp.zeros((STEP, NB), jnp.float32)


def cross_kernel(core, x, y, mine, other):
    half = N // 2
    for out, which in ((mine, core[0]), (other, 1 - core[0])):
        left = x[:, pl.ds(pl.multiple_of(which * half, half), half)]
        for j in range(KB // 2):
            prod = lax.dot_general(
                left, y[:, 2 * j * NB:2 * (j + 1) * NB], (((0,), (0,)), ((), ())), preferred_element_type=jnp.float32
            )
            for i in range(half // NB):
                for d in range(2):
                    out[i * KB // 2 + j, d * NB:(d + 1) * NB, :] = prod[i * NB:(i + 1) * NB, d * NB:(d + 1) * NB]


def exchange(pieces, axes):
    return lax.all_to_all(pieces, axes, 0, 0, tiled=True)


def spread(piece, n):
    return jnp.broadcast_to(piece[None], (n, *piece.shape))


def swap(a):
    return lax.ppermute(a, "core", [(0, 1), (1, 0)])


def shift(pieces, axis, size):
    return [
        lax.ppermute(p, axis, [(i, (i + k) % size) for i in range(size)]) if k else p for k, p in enumerate(pieces)
    ]


def plane_first_kernel(at, gram, gram_got, cross, cross_got, *outs):
    x, y, cut = at[0], at[1], PART // 2
    for k in range(4):
        for j in range(4):
            p = ((x + k) & 3) * 4 + j
            outs[k][j] = gram[p, :cut] + gram_got[p, :cut]
            p = j * 4 + ((y + k) & 3)
            outs[4 + k][j, :GRAM - cut] = gram[p, cut:] + gram_got[p, cut:]
            outs[4 + k][j, GRAM - cut:] = cross[p] + cross_got[p]


def plane_second_kernel(at, *refs):
    ins, outs = refs[:8], refs[8:]
    for k in range(4):
        for base, me in ((0, at[1]), (4, at[0])):
            p = (me + k) & 3
            outs[base + k][...] = (ins[base][p] + ins[base + 1][p]) + (ins[base + 2][p] + ins[base + 3][p])


def line_first_kernel(at, *refs):
    ins, outs = refs[:8], refs[8:]
    rows = PART // 8
    for k in range(4):
        lines = pl.ds(pl.multiple_of(((at[2] + k) & 3) * rows, 8), rows)
        for h in range(2):
            a, b, c, d = (r[lines, :] for r in ins[4 * h:4 * h + 4])
            outs[k][h] = (a + b) + (c + d)


def line_second_kernel(at, a, b, c, d, *outs):
    for k in range(2):
        h = (at[3] + k) & 1
        outs[k][...] = (a[h] + b[h]) + (c[h] + d[h])


def share_of_sum(at, gram, gram_got, cross, cross_got):
    half, rows = PART // 2, PART // 8
    pieces = call(plane_first_kernel, [(4, half, NB)] * 8, 1, 4)(at, gram, gram_got, cross, cross_got)
    got = shift(pieces[:4], "x", 4) + shift(pieces[4:], "y", 4)
    pieces = call(plane_second_kernel, [(half, NB)] * 8, 1, 8)(at, *got)
    got = shift(pieces[:4], "y", 4) + shift(pieces[4:], "x", 4)
    pieces = call(line_first_kernel, [(2, rows, NB)] * 4, 1, 8)(at, *got)
    got = shift(pieces, "z_lo", 4)
    mine, theirs = shift(call(line_second_kernel, [(rows, NB)] * 2, 1, 4)(at, *got), "z_hi", 2)
    return mine + theirs


def tile(v):
    return jnp.broadcast_to(v, (G, NB))


def pivots(s):
    l = [[None] * G for _ in range(G)]
    r = [None] * G
    for k in range(G):
        r[k] = lax.rsqrt(s[k][k])
        for j in range(k + 1, G):
            l[j][k] = s[k][j] * r[k]
        for i in range(k + 1, G):
            for j in range(i, G):
                s[i][j] = s[i][j] - l[i][k] * l[j][k]
    return l, r


def forward(l, r, rows):
    out = []
    for k in range(G):
        v = rows[k]
        for j in range(k):
            v = v - l[k][j] * out[j]
        out.append(v * r[k])
    return out


def factor_block(work):
    groups = SB // G
    for top in range(0, NB, SB):
        left = [work[top + G * g:top + G * (g + 1), :NB] for g in range(groups)]
        right = [work[top + G * g:top + G * (g + 1), NB:] for g in range(groups)]
        for p in range(groups):
            c0 = top + G * p
            s = [[tile(left[p][i:i + 1, c0 + j:c0 + j + 1]) if j >= i else None for j in range(G)] for i in range(G)]
            cols = [
                [jnp.broadcast_to(left[q][:, c0 + k:c0 + k + 1], (G, NB)) for k in range(G)]
                for q in range(p + 1, groups)
            ]
            l, r = pivots(s)
            u = forward(l, r, [tile(left[p][i:i + 1, :]) for i in range(G)])
            b = forward(l, r, [tile(right[p][i:i + 1, :]) for i in range(G)])
            for i in range(G):
                work[c0 + i:c0 + i + 1, :NB] = u[i][0:1]
                work[c0 + i:c0 + i + 1, NB:] = b[i][0:1]
            for q in range(p + 1, groups):
                lc = forward(l, r, cols[q - p - 1])
                for k in range(G):
                    left[q] = left[q] - lc[k] * u[k]
                    right[q] = right[q] - lc[k] * b[k]
        rest = top + SB
        if rest < NB:
            rows = work[top:rest, :]
            work[rest:, :] -= mm(rows[:, rest:NB], rows, ((0,), (0,)))


def eliminate(first, last, width, upper, inverse, work):
    eye = lax.broadcasted_iota(jnp.int32, (NB, NB), 0) == lax.broadcasted_iota(jnp.int32, (NB, NB), 1)

    def step(k, carry):
        at = pl.multiple_of(k * NB, NB)
        work[:, :NB] = upper[pl.ds(at, NB), pl.ds(at, NB)]
        work[:, NB:] = eye.astype(jnp.float32)
        factor_block(work)
        inverse[pl.ds(at, NB), :] = work[:, NB:]
        for kk in range(first, min(last, width - 1)):
            @pl.when(k == kk)
            def _():
                lo, nxt, end = kk * NB, (kk + 1) * NB, width * NB
                upper[lo:nxt, nxt:end] = mm(work[:, NB:], upper[lo:nxt, nxt:end], ((1,), (0,)))
                for i in range(kk + 1, width):
                    rows = upper[lo:nxt, i * NB:end]
                    upper[i * NB:(i + 1) * NB, i * NB:end] -= mm(rows[:, :NB], rows, ((0,), (0,)))
        return carry

    lax.fori_loop(first, last, step, 0)


def head_kernel(blocks, upper, inverse, work):
    for at, (i, j) in enumerate(EARLY):
        upper[i * NB:(i + 1) * NB, j * NB:(j + 1) * NB] = blocks[at * NB:(at + 1) * NB, :]
    eliminate(0, HEAD, HEAD, upper, inverse, work)


def tail_kernel(rows, blocks, head, head_inverse, upper, inverse, z, work):
    h = HEAD * NB
    upper[:h, :h] = head[...]
    inverse[:h, :] = head_inverse[...]
    for at, (i, j) in enumerate(LATE):
        upper[i * NB:(i + 1) * NB, j * NB:(j + 1) * NB] = blocks[at * NB:(at + 1) * NB, :]
    for k in range(HEAD):
        lo, nxt = k * NB, (k + 1) * NB
        v = upper[lo:nxt, h:]
        if k:
            v = v - mm(upper[:lo, lo:nxt], upper[:lo, h:], ((0,), (0,)))
        upper[lo:nxt, h:] = mm(inverse[lo:nxt, :], v, ((1,), (0,)))
    for i in range(HEAD, KB):
        done = upper[:h, i * NB:]
        upper[i * NB:(i + 1) * NB, i * NB:] -= mm(done[:, :NB], done, ((0,), (0,)))
    eliminate(HEAD, KB, KB, upper, inverse, work)
    line = lax.broadcasted_iota(jnp.int32, (G, NB), 0)
    want = jnp.where(line < OWNED, rows[0] + line, rows[1] + line - OWNED)
    lane = lax.broadcasted_iota(jnp.int32, (G, NB), 1)
    for k in reversed(range(KB)):
        v = (want == lane + k * NB).astype(jnp.float32)
        if k < KB - 1:
            v = v - mm(z[:, (k + 1) * NB:], upper[k * NB:(k + 1) * NB, (k + 1) * NB:], ((1,), (1,)))
        z[:, k * NB:(k + 1) * NB] = mm(v, inverse[k * NB:(k + 1) * NB, :], ((1,), (0,)))


def apply_kernel(core, z_own, z_sent, cross, out):
    half = N // 2
    z = jnp.where(core[0] == 0, z_own[:, :half], z_sent[:, half:])
    acc = jnp.zeros((G, N), jnp.float32)
    for i in range(half // NB):
        row = jnp.concatenate([cross[(i * KB + j) // 2, j % 2 * NB:(j % 2 + 1) * NB, :] for j in range(KB)], axis=1)
        acc = acc + mm(z[:, i * NB:(i + 1) * NB], row, ((1,), (0,)))
    out[...] = acc


def solve_kernel(w_own, w_sent, upper, inverse, y):
    w = w_own[...] + w_sent[...]
    for k in range(KB):
        v = w[:, k * NB:(k + 1) * NB]
        if k:
            v = v - mm(y[:, :k * NB], upper[:k * NB, k * NB:(k + 1) * NB], ((1,), (0,)))
        y[:, k * NB:(k + 1) * NB] = mm(v, inverse[k * NB:(k + 1) * NB, :], ((1,), (1,)))


def after(value, *others):
    return lax.optimization_barrier((value, *others))[0]


def on_device(view_x, view_y):
    core = lax.axis_index("core")
    core_ref = core.astype(jnp.int32).reshape(1)
    x, y, z_lo, z_hi = (lax.axis_index(a).astype(jnp.int32) for a in ("x", "y", "z_lo", "z_hi"))
    at = jnp.stack([x, y, z_lo, z_hi])
    chip = (z_hi * 4 + x) * 32 + y * 4 + z_lo
    rows = jnp.stack([chip * OWNED, (chip + 16) * OWNED])
    work = pltpu.VMEM((NB, 2 * NB), jnp.float32)

    with jax.named_scope("sums"):
        gram, gram_other = call(
            gram_kernel, [(16, GRAM, NB)] * 2, 1, 2, [pltpu.VMEM(view_x.shape, view_x.dtype)], flops=2 * 10**9
        )(core_ref, view_x, view_y)
        cross, cross_other = call(cross_kernel, [(16, PART - GRAM, NB)] * 2, 1, 2, flops=10**9)(
            core_ref, *after((view_x, view_y), gram)
        )
        share = share_of_sum(at, gram, swap(gram_other), cross, swap(cross_other))
    with jax.named_scope("early"):
        piece = exchange(spread(share, 8), LINE).reshape(PART, NB)
        early = exchange(spread(piece[:EARLY_ROWS], 16), PLANE).reshape(-1, NB)
    with jax.named_scope("late"):
        piece = after(piece, early)
        late = exchange(spread(piece[EARLY_ROWS:GRAM], 16), PLANE).reshape(-1, NB)
    with jax.named_scope("cross_back"):
        cross = exchange(spread(after(piece, late)[GRAM:], 16), PLANE)

    head, head_inverse = call(
        head_kernel, [(HEAD * NB, HEAD * NB), (HEAD * NB, NB)], 0, 1, [work], flops=3 * 10**10
    )(early)
    upper, inverse, z = call(tail_kernel, [(N, N), (N, NB), (G, N)], 1, 3, [work], flops=4 * 10**10)(
        rows, late, head, head_inverse
    )
    (w,) = call(apply_kernel, [(G, N)], 1, 3)(core_ref, z, swap(z), cross)
    (y_rows,) = call(solve_kernel, [(G, N)], 0, 4)(w, swap(w), upper, inverse)
    y_sent = swap(y_rows[:OWNED])
    return jnp.where(core == 0, y_sent, y_rows[OWNED:])


def solution(mesh):
    fine = Mesh(mesh.devices.reshape(SIZES), AXES)
    spec = P(AXES, None)
    return jax.shard_map(on_device, mesh=fine, in_specs=(spec, spec), out_specs=spec, check_vma=False)
```

```python
import functools

import jax
import jax.numpy as jnp
from jax import lax
from jax.experimental import pallas as pl
from jax.experimental.pallas import tpu as pltpu
from jax.sharding import Mesh
from jax.sharding import PartitionSpec as P

AXES = ("z_hi", "x", "core", "y", "z_lo")
SIZES = (2, 4, 2, 4, 4)
PLANE = ("x", "y")
LINE = ("z_hi", "z_lo")
N, NB, SB, G = 1024, 128, 32, 8
KB = N // NB
OWNED = 4
HEAD = 5
EARLY = [(i, j) for i in range(HEAD) for j in range(i, HEAD)]
LATE = [(i, j) for i in range(KB) for j in range(max(i, HEAD), KB)]
LATE_SLOTS = 40 - len(EARLY)
STEP = 8
EARLY_ROWS = len(EARLY) * NB // 16
GRAM = 40 * NB // 16
CROSS = N // 2 * N // NB // 16
VMEM = pl.BlockSpec(memory_space=pltpu.VMEM)
SMEM = pl.BlockSpec(memory_space=pltpu.SMEM)


def mm(a, b, dims):
    return lax.dot_general(
        a, b, (dims, ((), ())), precision=lax.Precision.HIGHEST, preferred_element_type=jnp.float32
    )


def call(kernel, outs, n_smem, n_vmem, scratch=(), flops=0, bytes_accessed=0):
    return pl.pallas_call(
        kernel,
        out_shape=[jax.ShapeDtypeStruct(s, jnp.float32) for s in outs],
        in_specs=[SMEM] * n_smem + [VMEM] * n_vmem,
        out_specs=[VMEM] * len(outs),
        scratch_shapes=list(scratch),
        compiler_params=pltpu.CompilerParams(vmem_limit_bytes=16 << 20),
        cost_estimate=pl.CostEstimate(flops=flops, bytes_accessed=bytes_accessed, transcendentals=0),
    )


def gram_kernel(core, x, y, mine, other, pick):
    early_rows, late_rows = EARLY_ROWS, GRAM - EARLY_ROWS
    for out, which in ((mine, 0), (other, 1)):
        @pl.when(core[0] == which)
        def _():
            pick[...] = x[...]

        @pl.when(core[0] != which)
        def _():
            pick[...] = y[...]

        for i in range(KB):
            prod = lax.dot_general(
                pick[:, i * NB:(i + 1) * NB], pick[:, i * NB:], (((0,), (0,)), ((), ())),
                preferred_element_type=jnp.float32,
            )
            for j in range(i, KB):
                early = (i, j) in EARLY
                at = (EARLY if early else LATE).index((i, j)) * NB
                rows, base = (early_rows, 0) if early else (late_rows, early_rows)
                for t in range(0, NB, STEP):
                    part, line = divmod(at + t, rows)
                    out[part, base + line:base + line + STEP, :] = prod[t:t + STEP, (j - i) * NB:(j - i + 1) * NB]
        for at in range(len(LATE) * NB, LATE_SLOTS * NB, STEP):
            part, line = divmod(at, late_rows)
            out[part, early_rows + line:early_rows + line + STEP, :] = jnp.zeros((STEP, NB), jnp.float32)


def cross_kernel(core, x, y, mine, other):
    half = N // 2
    for out, which in ((mine, core[0]), (other, 1 - core[0])):
        left = x[:, pl.ds(pl.multiple_of(which * half, half), half)]
        for j in range(KB // 2):
            prod = lax.dot_general(
                left, y[:, 2 * j * NB:2 * (j + 1) * NB], (((0,), (0,)), ((), ())), preferred_element_type=jnp.float32
            )
            for i in range(half // NB):
                for d in range(2):
                    out[i * KB // 2 + j, d * NB:(d + 1) * NB, :] = prod[i * NB:(i + 1) * NB, d * NB:(d + 1) * NB]


def exchange(pieces, axes):
    return lax.all_to_all(pieces, axes, 0, 0, tiled=True)


def spread(piece, n):
    return jnp.broadcast_to(piece[None], (n, *piece.shape))


def swap(a):
    return lax.ppermute(a, "core", [(0, 1), (1, 0)])


def shift(pieces, axis, size):
    return [
        lax.ppermute(p, axis, [(i, (i + k) % size) for i in range(size)]) if k else p for k, p in enumerate(pieces)
    ]


def plane_first_kernel(at, own, got, *outs):
    cut = own.shape[1] // 2
    for k in range(4):
        for j in range(4):
            p = ((at[0] + k) & 3) * 4 + j
            outs[k][j] = own[p, :cut] + got[p, :cut]
            p = j * 4 + ((at[1] + k) & 3)
            outs[4 + k][j] = own[p, cut:] + got[p, cut:]


def plane_second_kernel(at, *refs):
    ins, outs = refs[:8], refs[8:]
    for k in range(4):
        for base, me in ((0, at[1]), (4, at[0])):
            p = (me + k) & 3
            outs[base + k][...] = (ins[base][p] + ins[base + 1][p]) + (ins[base + 2][p] + ins[base + 3][p])


def line_first_kernel(at, *refs):
    ins, outs = refs[:8], refs[8:]
    rows = ins[0].shape[0] // 4
    for k in range(4):
        lines = pl.ds(pl.multiple_of(((at[2] + k) & 3) * rows, 8), rows)
        for h in range(2):
            a, b, c, d = (r[lines, :] for r in ins[4 * h:4 * h + 4])
            outs[k][h] = (a + b) + (c + d)


def line_second_kernel(at, a, b, c, d, *outs):
    for k in range(2):
        h = (at[3] + k) & 1
        outs[k][...] = (a[h] + b[h]) + (c[h] + d[h])


def sum_kernel(*refs):
    total = refs[0][...]
    for r in refs[1:-1]:
        total = total + r[...]
    refs[-1][...] = total


def sum_and_spread_kernel(a, b, out):
    out[...] = jnp.broadcast_to((a[...] + b[...])[None], out.shape)


def plane_total_kernel(*refs):
    ins, out = refs[:8], refs[8]
    cut = out.shape[0] // 2
    for h in range(2):
        a, b, c, d = (r[...] for r in ins[4 * h:4 * h + 4])
        out[h * cut:(h + 1) * cut, :] = (a + b) + (c + d)


def plane_first(at, own, got):
    pieces = call(plane_first_kernel, [(4, own.shape[1] // 2, NB)] * 8, 1, 2)(at, own, got)
    return shift(pieces[:4], "x", 4) + shift(pieces[4:], "y", 4)


def plane_second_pieces(at, got):
    return call(plane_second_kernel, [got[0].shape[1:]] * 8, 1, 8)(at, *got)


def plane_second_shift(pieces):
    return shift(pieces[:4], "y", 4) + shift(pieces[4:], "x", 4)


def tile(v):
    return jnp.broadcast_to(v, (G, NB))


def pivots(s):
    l = [[None] * G for _ in range(G)]
    r = [None] * G
    for k in range(G):
        r[k] = lax.rsqrt(s[k][k])
        for j in range(k + 1, G):
            l[j][k] = s[k][j] * r[k]
        for i in range(k + 1, G):
            for j in range(i, G):
                s[i][j] = s[i][j] - l[i][k] * l[j][k]
    return l, r


def forward(l, r, rows):
    out = []
    for k in range(G):
        v = rows[k]
        for j in range(k):
            v = v - l[k][j] * out[j]
        out.append(v * r[k])
    return out


def factor_block(work):
    groups = SB // G
    for top in range(0, NB, SB):
        left = [work[top + G * g:top + G * (g + 1), :NB] for g in range(groups)]
        right = [work[top + G * g:top + G * (g + 1), NB:] for g in range(groups)]
        for p in range(groups):
            c0 = top + G * p
            s = [[tile(left[p][i:i + 1, c0 + j:c0 + j + 1]) if j >= i else None for j in range(G)] for i in range(G)]
            cols = [
                [jnp.broadcast_to(left[q][:, c0 + k:c0 + k + 1], (G, NB)) for k in range(G)]
                for q in range(p + 1, groups)
            ]
            l, r = pivots(s)
            u = forward(l, r, [tile(left[p][i:i + 1, :]) for i in range(G)])
            b = forward(l, r, [tile(right[p][i:i + 1, :]) for i in range(G)])
            for i in range(G):
                work[c0 + i:c0 + i + 1, :NB] = u[i][0:1]
                work[c0 + i:c0 + i + 1, NB:] = b[i][0:1]
            for q in range(p + 1, groups):
                lc = forward(l, r, cols[q - p - 1])
                for k in range(G):
                    left[q] = left[q] - lc[k] * u[k]
                    right[q] = right[q] - lc[k] * b[k]
        rest = top + SB
        if rest < NB:
            rows = work[top:rest, :]
            work[rest:, :] -= mm(rows[:, rest:NB], rows, ((0,), (0,)))


def eliminate(first, last, width, upper, inverse, work):
    eye = lax.broadcasted_iota(jnp.int32, (NB, NB), 0) == lax.broadcasted_iota(jnp.int32, (NB, NB), 1)

    def step(k, carry):
        at = pl.multiple_of(k * NB, NB)
        work[:, :NB] = upper[pl.ds(at, NB), pl.ds(at, NB)]
        work[:, NB:] = eye.astype(jnp.float32)
        factor_block(work)
        inverse[pl.ds(at, NB), :] = work[:, NB:]
        for kk in range(first, min(last, width - 1)):
            @pl.when(k == kk)
            def _():
                lo, nxt, end = kk * NB, (kk + 1) * NB, width * NB
                upper[lo:nxt, nxt:end] = mm(work[:, NB:], upper[lo:nxt, nxt:end], ((1,), (0,)))
                for i in range(kk + 1, width):
                    rows = upper[lo:nxt, i * NB:end]
                    upper[i * NB:(i + 1) * NB, i * NB:end] -= mm(rows[:, :NB], rows, ((0,), (0,)))
        return carry

    lax.fori_loop(first, last, step, 0)


def head_kernel(last, blocks, upper, inverse, work):
    for at, (i, j) in enumerate(EARLY):
        upper[i * NB:(i + 1) * NB, j * NB:(j + 1) * NB] = blocks[at * NB:(at + 1) * NB, :]
    eliminate(0, last, HEAD, upper, inverse, work)


def neck_kernel(first, last, upper_in, inverse_in, upper, inverse, work):
    upper[...] = upper_in[...]
    inverse[...] = inverse_in[...]
    eliminate(first, last, HEAD, upper, inverse, work)


def tail_kernel(rows, blocks, head, head_inverse, upper, inverse, z, work):
    h = HEAD * NB
    upper[:h, :h] = head[...]
    inverse[:h, :] = head_inverse[...]
    for at, (i, j) in enumerate(LATE):
        upper[i * NB:(i + 1) * NB, j * NB:(j + 1) * NB] = blocks[at * NB:(at + 1) * NB, :]
    for k in range(HEAD):
        lo, nxt = k * NB, (k + 1) * NB
        v = upper[lo:nxt, h:]
        if k:
            v = v - mm(upper[:lo, lo:nxt], upper[:lo, h:], ((0,), (0,)))
        upper[lo:nxt, h:] = mm(inverse[lo:nxt, :], v, ((1,), (0,)))
    for i in range(HEAD, KB):
        done = upper[:h, i * NB:]
        upper[i * NB:(i + 1) * NB, i * NB:] -= mm(done[:, :NB], done, ((0,), (0,)))
    eliminate(HEAD, KB, KB, upper, inverse, work)
    line = lax.broadcasted_iota(jnp.int32, (G, NB), 0)
    want = jnp.where(line < OWNED, rows[0] + line, rows[1] + line - OWNED)
    lane = lax.broadcasted_iota(jnp.int32, (G, NB), 1)
    for k in reversed(range(KB)):
        v = (want == lane + k * NB).astype(jnp.float32)
        if k < KB - 1:
            v = v - mm(z[:, (k + 1) * NB:], upper[k * NB:(k + 1) * NB, (k + 1) * NB:], ((1,), (1,)))
        z[:, k * NB:(k + 1) * NB] = mm(v, inverse[k * NB:(k + 1) * NB, :], ((1,), (0,)))


def apply_kernel(core, z_own, z_sent, cross, out):
    half = N // 2
    z = jnp.where(core[0] == 0, z_own[:, :half], z_sent[:, half:])
    acc = jnp.zeros((G, N), jnp.float32)
    for i in range(half // NB):
        row = jnp.concatenate([cross[(i * KB + j) // 2, j % 2 * NB:(j % 2 + 1) * NB, :] for j in range(KB)], axis=1)
        acc = acc + mm(z[:, i * NB:(i + 1) * NB], row, ((1,), (0,)))
    out[...] = acc


def solve_kernel(w_own, w_sent, upper, inverse, y):
    w = w_own[...] + w_sent[...]
    for k in range(KB):
        v = w[:, k * NB:(k + 1) * NB]
        if k:
            v = v - mm(y[:, :k * NB], upper[:k * NB, k * NB:(k + 1) * NB], ((1,), (0,)))
        y[:, k * NB:(k + 1) * NB] = mm(v, inverse[k * NB:(k + 1) * NB, :], ((1,), (1,)))


def after(value, *others):
    return lax.optimization_barrier((value, *others))[0]


def on_device(view_x, view_y):
    core = lax.axis_index("core")
    core_ref = core.astype(jnp.int32).reshape(1)
    x, y, z_lo, z_hi = (lax.axis_index(a).astype(jnp.int32) for a in ("x", "y", "z_lo", "z_hi"))
    at = jnp.stack([x, y, z_lo, z_hi])
    chip = (z_hi * 4 + x) * 32 + y * 4 + z_lo
    rows = jnp.stack([chip * OWNED, (chip + 16) * OWNED])
    work = pltpu.VMEM((NB, 2 * NB), jnp.float32)

    gram, gram_other = call(
        gram_kernel, [(16, GRAM, NB)] * 2, 1, 2, [pltpu.VMEM(view_x.shape, view_x.dtype)], flops=2 * 10**9
    )(core_ref, view_x, view_y)
    cross, cross_other = call(cross_kernel, [(16, CROSS, NB)] * 2, 1, 2, flops=10**9)(
        core_ref, *after((view_x, view_y), gram)
    )
    with jax.named_scope("gram_out"):
        got = plane_second_shift(plane_second_pieces(at, plane_first(at, gram, swap(gram_other))))
        lines = call(line_first_kernel, [(2, GRAM // 8, NB)] * 4, 1, 8)(at, *got)
        got = shift(lines, "z_lo", 4)
        mine, theirs = shift(call(line_second_kernel, [(GRAM // 8, NB)] * 2, 1, 4)(at, *got), "z_hi", 2)
        share = mine + theirs
    with jax.named_scope("cross_first"):
        cross_got = plane_first(at, *after((cross, swap(cross_other)), lines))
    with jax.named_scope("gram_back"):
        piece = exchange(spread(after(share, cross_got[1:4]), 8), LINE).reshape(GRAM, NB)
        early_wide, late_wide = spread(after(piece, cross_got)[:EARLY_ROWS], 16), spread(piece[EARLY_ROWS:], 16)
        early = exchange(early_wide, PLANE)
    with jax.named_scope("cross_second"):
        pieces = plane_second_pieces(at, after(cross_got, piece))
    with jax.named_scope("gram_back"):
        late = exchange(after(late_wide, early, pieces), PLANE).reshape(-1, NB)
        early = early.reshape(-1, NB)
    with jax.named_scope("cross_second"):
        cross_got = plane_second_shift(pieces)

    size = HEAD * NB
    shapes = [(size, size), (size, NB)]
    head = call(functools.partial(head_kernel, 2), shapes, 0, 1, [work], flops=10**9)(early)
    with jax.named_scope("cross_third"):
        (cross,) = call(plane_total_kernel, [(CROSS, NB)], 0, 8)(*after(cross_got, head))
        got = shift([cross] * 4, "z_lo", 4)
    head = call(functools.partial(neck_kernel, 2, 4), shapes, 0, 2, [work], flops=10**9)(*head)
    with jax.named_scope("cross_fourth"):
        (cross,) = call(sum_kernel, [(CROSS, NB)], 0, 4)(*after(got, head))
        cross, theirs = shift([cross] * 2, "z_hi", 2)
    head = call(functools.partial(neck_kernel, 4, 5), shapes, 0, 2, [work], flops=10**9)(*head)
    with jax.named_scope("cross_back"):
        (cross,) = call(sum_and_spread_kernel, [(16, CROSS, NB)], 0, 2)(*after((cross, theirs), head))
        cross = exchange(after(cross, late), PLANE)
    upper, inverse, z = call(tail_kernel, [(N, N), (N, NB), (G, N)], 1, 3, [work], flops=4 * 10**10)(rows, late, *head)
    (w,) = call(apply_kernel, [(G, N)], 1, 3)(core_ref, z, swap(z), cross)
    (y_rows,) = call(solve_kernel, [(G, N)], 0, 4)(w, swap(w), upper, inverse)
    y_sent = swap(y_rows[:OWNED])
    return jnp.where(core == 0, y_sent, y_rows[OWNED:])


def solution(mesh):
    fine = Mesh(mesh.devices.reshape(SIZES), AXES)
    spec = P(AXES, None)
    return jax.shard_map(on_device, mesh=fine, in_specs=(spec, spec), out_specs=spec, check_vma=False)
```

```python
import functools

import jax
import jax.numpy as jnp
from jax import lax
from jax.experimental import pallas as pl
from jax.experimental.pallas import tpu as pltpu
from jax.sharding import Mesh
from jax.sharding import PartitionSpec as P

AXES = ("z_hi", "x", "core", "y", "z_lo")
SIZES = (2, 4, 2, 4, 4)
PLANE = ("x", "y")
LINE = ("z_hi", "z_lo")
N, NB, SB, G = 1024, 128, 32, 8
KB = N // NB
OWNED = 4
HEAD = 5
EARLY = [(i, j) for i in range(HEAD) for j in range(i, HEAD)]
LATE = [(i, j) for i in range(KB) for j in range(max(i, HEAD), KB)]
LATE_SLOTS = 40 - len(EARLY)
STEP = 8
EARLY_ROWS = len(EARLY) * NB // 16
GRAM = 40 * NB // 16
PART = GRAM + N // 2 * N // NB // 16
VMEM = pl.BlockSpec(memory_space=pltpu.VMEM)
SMEM = pl.BlockSpec(memory_space=pltpu.SMEM)


def mm(a, b, dims):
    return lax.dot_general(
        a, b, (dims, ((), ())), precision=lax.Precision.HIGHEST, preferred_element_type=jnp.float32
    )


def call(kernel, outs, n_smem, n_vmem, scratch=(), flops=0, bytes_accessed=0):
    return pl.pallas_call(
        kernel,
        out_shape=[jax.ShapeDtypeStruct(s, jnp.float32) for s in outs],
        in_specs=[SMEM] * n_smem + [VMEM] * n_vmem,
        out_specs=[VMEM] * len(outs),
        scratch_shapes=list(scratch),
        compiler_params=pltpu.CompilerParams(vmem_limit_bytes=16 << 20),
        cost_estimate=pl.CostEstimate(flops=flops, bytes_accessed=bytes_accessed, transcendentals=0),
    )


def gram_kernel(core, x, y, mine, other, pick):
    early_rows, late_rows = EARLY_ROWS, GRAM - EARLY_ROWS
    for out, which in ((mine, 0), (other, 1)):
        @pl.when(core[0] == which)
        def _():
            pick[...] = x[...]

        @pl.when(core[0] != which)
        def _():
            pick[...] = y[...]

        for i in range(KB):
            prod = lax.dot_general(
                pick[:, i * NB:(i + 1) * NB], pick[:, i * NB:], (((0,), (0,)), ((), ())),
                preferred_element_type=jnp.float32,
            )
            for j in range(i, KB):
                early = (i, j) in EARLY
                at = (EARLY if early else LATE).index((i, j)) * NB
                rows, base = (early_rows, 0) if early else (late_rows, early_rows)
                for t in range(0, NB, STEP):
                    part, line = divmod(at + t, rows)
                    out[part, base + line:base + line + STEP, :] = prod[t:t + STEP, (j - i) * NB:(j - i + 1) * NB]
        for at in range(len(LATE) * NB, LATE_SLOTS * NB, STEP):
            part, line = divmod(at, late_rows)
            out[part, early_rows + line:early_rows + line + STEP, :] = jnp.zeros((STEP, NB), jnp.float32)


def cross_kernel(core, x, y, mine, other):
    half = N // 2
    for out, which in ((mine, core[0]), (other, 1 - core[0])):
        left = x[:, pl.ds(pl.multiple_of(which * half, half), half)]
        for j in range(KB // 2):
            prod = lax.dot_general(
                left, y[:, 2 * j * NB:2 * (j + 1) * NB], (((0,), (0,)), ((), ())), preferred_element_type=jnp.float32
            )
            for i in range(half // NB):
                for d in range(2):
                    out[i * KB // 2 + j, d * NB:(d + 1) * NB, :] = prod[i * NB:(i + 1) * NB, d * NB:(d + 1) * NB]


def exchange(pieces, axes):
    return lax.all_to_all(pieces, axes, 0, 0, tiled=True)


def spread(piece, n):
    return jnp.broadcast_to(piece[None], (n, *piece.shape))


def swap(a):
    return lax.ppermute(a, "core", [(0, 1), (1, 0)])


def plane_route(k, step):
    return [
        ((x * 2 + c) * 4 + y, ((x + k) % 4 * 2 + c) * 4 + y if c == step else (x * 2 + c) * 4 + (y + k) % 4)
        for x in range(4) for c in range(2) for y in range(4)
    ]


def shift(pieces, axes, route):
    return [lax.ppermute(p, axes, route(k)) if k else p for k, p in enumerate(pieces)]


def along_plane(pieces, step):
    return shift(pieces, ("x", "core", "y"), lambda k: plane_route(k, step))


def along_line(pieces, axis):
    size = len(pieces)
    return shift(pieces, axis, lambda k: [(i, (i + k) % size) for i in range(size)])


def plane_first_kernel(at, gram, gram_got, cross, cross_got, *outs):
    for k in range(4):
        for j in range(4):
            p = ((at[0] + k) & 3) * at[2] + j * at[3]
            outs[k][j, :GRAM] = gram[p] + gram_got[p]
            outs[k][j, GRAM:] = cross[p] + cross_got[p]


def plane_second_kernel(at, a, b, c, d, *outs):
    for k in range(4):
        p = (at[1] + k) & 3
        outs[k][...] = (a[p] + b[p]) + (c[p] + d[p])


def line_first_kernel(at, *refs):
    ins, outs = refs[:4], refs[4:]
    rows = PART // 8
    for k in range(4):
        for h in range(2):
            start = (h * 4 + ((at[4] + k) & 3)) * rows
            lines = pl.ds(pl.multiple_of(start, 8), rows)
            a, b, c, d = (r[lines, :] for r in ins)
            outs[k][h] = (a + b) + (c + d)


def line_second_kernel(at, a, b, c, d, *outs):
    for k in range(2):
        h = (at[5] + k) & 1
        outs[k][...] = (a[h] + b[h]) + (c[h] + d[h])


def share_of_sum(at, gram, gram_got, cross, cross_got):
    rows = PART // 8
    pieces = call(plane_first_kernel, [(4, PART, NB)] * 4, 1, 4)(at, gram, gram_got, cross, cross_got)
    pieces = call(plane_second_kernel, [(PART, NB)] * 4, 1, 4)(at, *along_plane(pieces, 0))
    pieces = call(line_first_kernel, [(2, rows, NB)] * 4, 1, 4)(at, *along_plane(pieces, 1))
    pieces = call(line_second_kernel, [(rows, NB)] * 2, 1, 4)(at, *along_line(pieces, "z_lo"))
    mine, theirs = along_line(pieces, "z_hi")
    return mine + theirs


def tile(v):
    return jnp.broadcast_to(v, (G, NB))


def pivots(s):
    l = [[None] * G for _ in range(G)]
    r = [None] * G
    for k in range(G):
        r[k] = lax.rsqrt(s[k][k])
        for j in range(k + 1, G):
            l[j][k] = s[k][j] * r[k]
        for i in range(k + 1, G):
            for j in range(i, G):
                s[i][j] = s[i][j] - l[i][k] * l[j][k]
    return l, r


def forward(l, r, rows):
    out = []
    for k in range(G):
        v = rows[k]
        for j in range(k):
            v = v - l[k][j] * out[j]
        out.append(v * r[k])
    return out


def factor_block(work):
    groups = SB // G
    for top in range(0, NB, SB):
        left = [work[top + G * g:top + G * (g + 1), :NB] for g in range(groups)]
        right = [work[top + G * g:top + G * (g + 1), NB:] for g in range(groups)]
        for p in range(groups):
            c0 = top + G * p
            s = [[tile(left[p][i:i + 1, c0 + j:c0 + j + 1]) if j >= i else None for j in range(G)] for i in range(G)]
            cols = [
                [jnp.broadcast_to(left[q][:, c0 + k:c0 + k + 1], (G, NB)) for k in range(G)]
                for q in range(p + 1, groups)
            ]
            l, r = pivots(s)
            u = forward(l, r, [tile(left[p][i:i + 1, :]) for i in range(G)])
            b = forward(l, r, [tile(right[p][i:i + 1, :]) for i in range(G)])
            for i in range(G):
                work[c0 + i:c0 + i + 1, :NB] = u[i][0:1]
                work[c0 + i:c0 + i + 1, NB:] = b[i][0:1]
            for q in range(p + 1, groups):
                lc = forward(l, r, cols[q - p - 1])
                for k in range(G):
                    left[q] = left[q] - lc[k] * u[k]
                    right[q] = right[q] - lc[k] * b[k]
        rest = top + SB
        if rest < NB:
            rows = work[top:rest, :]
            work[rest:, :] -= mm(rows[:, rest:NB], rows, ((0,), (0,)))


def eliminate(first, last, width, upper, inverse, work):
    eye = lax.broadcasted_iota(jnp.int32, (NB, NB), 0) == lax.broadcasted_iota(jnp.int32, (NB, NB), 1)

    def step(k, carry):
        at = pl.multiple_of(k * NB, NB)
        work[:, :NB] = upper[pl.ds(at, NB), pl.ds(at, NB)]
        work[:, NB:] = eye.astype(jnp.float32)
        factor_block(work)
        inverse[pl.ds(at, NB), :] = work[:, NB:]
        for kk in range(first, min(last, width - 1)):
            @pl.when(k == kk)
            def _():
                lo, nxt, end = kk * NB, (kk + 1) * NB, width * NB
                upper[lo:nxt, nxt:end] = mm(work[:, NB:], upper[lo:nxt, nxt:end], ((1,), (0,)))
                for i in range(kk + 1, width):
                    rows = upper[lo:nxt, i * NB:end]
                    upper[i * NB:(i + 1) * NB, i * NB:end] -= mm(rows[:, :NB], rows, ((0,), (0,)))
        return carry

    lax.fori_loop(first, last, step, 0)


def head_kernel(blocks, upper, inverse, work):
    for at, (i, j) in enumerate(EARLY):
        upper[i * NB:(i + 1) * NB, j * NB:(j + 1) * NB] = blocks[at * NB:(at + 1) * NB, :]
    eliminate(0, HEAD, HEAD, upper, inverse, work)


def tail_kernel(rows, blocks, head, head_inverse, upper, inverse, z, work):
    h = HEAD * NB
    upper[:h, :h] = head[...]
    inverse[:h, :] = head_inverse[...]
    for at, (i, j) in enumerate(LATE):
        upper[i * NB:(i + 1) * NB, j * NB:(j + 1) * NB] = blocks[at * NB:(at + 1) * NB, :]
    for k in range(HEAD):
        lo, nxt = k * NB, (k + 1) * NB
        v = upper[lo:nxt, h:]
        if k:
            v = v - mm(upper[:lo, lo:nxt], upper[:lo, h:], ((0,), (0,)))
        upper[lo:nxt, h:] = mm(inverse[lo:nxt, :], v, ((1,), (0,)))
    for i in range(HEAD, KB):
        done = upper[:h, i * NB:]
        upper[i * NB:(i + 1) * NB, i * NB:] -= mm(done[:, :NB], done, ((0,), (0,)))
    eliminate(HEAD, KB, KB, upper, inverse, work)
    line = lax.broadcasted_iota(jnp.int32, (G, NB), 0)
    want = jnp.where(line < OWNED, rows[0] + line, rows[1] + line - OWNED)
    lane = lax.broadcasted_iota(jnp.int32, (G, NB), 1)
    for k in reversed(range(KB)):
        v = (want == lane + k * NB).astype(jnp.float32)
        if k < KB - 1:
            v = v - mm(z[:, (k + 1) * NB:], upper[k * NB:(k + 1) * NB, (k + 1) * NB:], ((1,), (1,)))
        z[:, k * NB:(k + 1) * NB] = mm(v, inverse[k * NB:(k + 1) * NB, :], ((1,), (0,)))


def apply_kernel(core, z_own, z_sent, cross, out):
    half = N // 2
    z = jnp.where(core[0] == 0, z_own[:, :half], z_sent[:, half:])
    acc = jnp.zeros((G, N), jnp.float32)
    for i in range(half // NB):
        row = jnp.concatenate([cross[(i * KB + j) // 2, j % 2 * NB:(j % 2 + 1) * NB, :] for j in range(KB)], axis=1)
        acc = acc + mm(z[:, i * NB:(i + 1) * NB], row, ((1,), (0,)))
    out[...] = acc


def solve_kernel(w_own, w_sent, upper, inverse, y):
    w = w_own[...] + w_sent[...]
    for k in range(KB):
        v = w[:, k * NB:(k + 1) * NB]
        if k:
            v = v - mm(y[:, :k * NB], upper[:k * NB, k * NB:(k + 1) * NB], ((1,), (0,)))
        y[:, k * NB:(k + 1) * NB] = mm(v, inverse[k * NB:(k + 1) * NB, :], ((1,), (1,)))


def after(value, *others):
    return lax.optimization_barrier((value, *others))[0]


def on_device(view_x, view_y):
    core = lax.axis_index("core")
    core_ref = core.astype(jnp.int32).reshape(1)
    x, y, z_lo, z_hi = (lax.axis_index(a).astype(jnp.int32) for a in ("x", "y", "z_lo", "z_hi"))
    at = jnp.stack([*jnp.where(core == 0, jnp.array([x, y, 4, 1]), jnp.array([y, x, 1, 4])), z_lo, z_hi]).astype(jnp.int32)
    chip = (z_hi * 4 + x) * 32 + y * 4 + z_lo
    rows = jnp.stack([chip * OWNED, (chip + 16) * OWNED])
    work = pltpu.VMEM((NB, 2 * NB), jnp.float32)

    with jax.named_scope("sums"):
        gram, gram_other = call(
            gram_kernel, [(16, GRAM, NB)] * 2, 1, 2, [pltpu.VMEM(view_x.shape, view_x.dtype)], flops=2 * 10**9
        )(core_ref, view_x, view_y)
        cross, cross_other = call(cross_kernel, [(16, PART - GRAM, NB)] * 2, 1, 2, flops=10**9)(
            core_ref, *after((view_x, view_y), gram)
        )
        share = share_of_sum(at, gram, swap(gram_other), cross, swap(cross_other))
    with jax.named_scope("back"):
        piece = exchange(spread(share, 8), LINE).reshape(PART, NB)
        early, late, cross = (
            spread(piece[lo:hi], 16) for lo, hi in ((0, EARLY_ROWS), (EARLY_ROWS, GRAM), (GRAM, PART))
        )
        early = after(exchange(early, PLANE), late, cross)
        late = exchange(after(late, early), PLANE)
        cross = exchange(after(cross, late), PLANE)
        early, late = early.reshape(-1, NB), late.reshape(-1, NB)

    head, head_inverse = call(
        head_kernel, [(HEAD * NB, HEAD * NB), (HEAD * NB, NB)], 0, 1, [work], flops=3 * 10**10
    )(early)
    upper, inverse, z = call(tail_kernel, [(N, N), (N, NB), (G, N)], 1, 3, [work], flops=4 * 10**10)(
        rows, late, head, head_inverse
    )
    (w,) = call(apply_kernel, [(G, N)], 1, 3)(core_ref, z, swap(z), cross)
    (y_rows,) = call(solve_kernel, [(G, N)], 0, 4)(w, swap(w), upper, inverse)
    y_sent = swap(y_rows[:OWNED])
    return jnp.where(core == 0, y_sent, y_rows[OWNED:])


def solution(mesh):
    fine = Mesh(mesh.devices.reshape(SIZES), AXES)
    spec = P(AXES, None)
    return jax.shard_map(on_device, mesh=fine, in_specs=(spec, spec), out_specs=spec, check_vma=False)
```

```python
import functools

import jax
import jax.numpy as jnp
from jax import lax
from jax.experimental import pallas as pl
from jax.experimental.pallas import tpu as pltpu
from jax.sharding import Mesh
from jax.sharding import PartitionSpec as P

AXES = ("z_hi", "x", "core", "y", "z_lo")
SIZES = (2, 4, 2, 4, 4)
PLANE = ("x", "y")
N, NB, SB, G = 1024, 128, 32, 8
KB = N // NB
OWNED = 4
HEAD = 5
EARLY = [(i, j) for i in range(HEAD) for j in range(i, HEAD)]
LATE = [(i, j) for i in range(KB) for j in range(max(i, HEAD), KB)]
LATE_SLOTS = 40 - len(EARLY)
STEP = 8
EARLY_ROWS = len(EARLY) * NB // 16
GRAM = 40 * NB // 16
PART = GRAM + N // 2 * N // NB // 16
VMEM = pl.BlockSpec(memory_space=pltpu.VMEM)
SMEM = pl.BlockSpec(memory_space=pltpu.SMEM)


def mm(a, b, dims):
    return lax.dot_general(
        a, b, (dims, ((), ())), precision=lax.Precision.HIGHEST, preferred_element_type=jnp.float32
    )


def call(kernel, outs, n_smem, n_vmem, scratch=(), flops=0, bytes_accessed=0):
    return pl.pallas_call(
        kernel,
        out_shape=[jax.ShapeDtypeStruct(s, jnp.float32) for s in outs],
        in_specs=[SMEM] * n_smem + [VMEM] * n_vmem,
        out_specs=[VMEM] * len(outs),
        scratch_shapes=list(scratch),
        compiler_params=pltpu.CompilerParams(vmem_limit_bytes=16 << 20),
        cost_estimate=pl.CostEstimate(flops=flops, bytes_accessed=bytes_accessed, transcendentals=0),
    )


def gram_kernel(core, x, y, mine, other, pick):
    early_rows, late_rows = EARLY_ROWS, GRAM - EARLY_ROWS
    for out, which in ((mine, 0), (other, 1)):
        @pl.when(core[0] == which)
        def _():
            pick[...] = x[...]

        @pl.when(core[0] != which)
        def _():
            pick[...] = y[...]

        for i in range(KB):
            prod = lax.dot_general(
                pick[:, i * NB:(i + 1) * NB], pick[:, i * NB:], (((0,), (0,)), ((), ())),
                preferred_element_type=jnp.float32,
            )
            for j in range(i, KB):
                early = (i, j) in EARLY
                at = (EARLY if early else LATE).index((i, j)) * NB
                rows, base = (early_rows, 0) if early else (late_rows, early_rows)
                for t in range(0, NB, STEP):
                    part, line = divmod(at + t, rows)
                    out[part, base + line:base + line + STEP, :] = prod[t:t + STEP, (j - i) * NB:(j - i + 1) * NB]
        for at in range(len(LATE) * NB, LATE_SLOTS * NB, STEP):
            part, line = divmod(at, late_rows)
            out[part, early_rows + line:early_rows + line + STEP, :] = jnp.zeros((STEP, NB), jnp.float32)


def cross_kernel(core, x, y, mine, other):
    half = N // 2
    for out, which in ((mine, core[0]), (other, 1 - core[0])):
        left = x[:, pl.ds(pl.multiple_of(which * half, half), half)]
        for j in range(KB // 2):
            prod = lax.dot_general(
                left, y[:, 2 * j * NB:2 * (j + 1) * NB], (((0,), (0,)), ((), ())), preferred_element_type=jnp.float32
            )
            for i in range(half // NB):
                for d in range(2):
                    out[i * KB // 2 + j, d * NB:(d + 1) * NB, :] = prod[i * NB:(i + 1) * NB, d * NB:(d + 1) * NB]


def exchange(pieces, axes):
    return lax.all_to_all(pieces, axes, 0, 0, tiled=True)


def swap(a):
    return lax.ppermute(a, "core", [(0, 1), (1, 0)])


def plane_route(k, step):
    return [
        ((x * 2 + c) * 4 + y, ((x + k) % 4 * 2 + c) * 4 + y if c == step else (x * 2 + c) * 4 + (y + k) % 4)
        for x in range(4) for c in range(2) for y in range(4)
    ]


def shift(pieces, axes, route):
    return [lax.ppermute(p, axes, route(k)) if k else p for k, p in enumerate(pieces)]


def along_plane(pieces, step):
    return shift(pieces, ("x", "core", "y"), lambda k: plane_route(k, step))


def along_line(pieces, axis):
    size = len(pieces)
    return shift(pieces, axis, lambda k: [(i, (i + k) % size) for i in range(size)])


def plane_first_kernel(at, gram, gram_got, cross, cross_got, *outs):
    for k in range(4):
        for j in range(4):
            p = ((at[0] + k) & 3) * at[2] + j * at[3]
            outs[k][j, :GRAM] = gram[p] + gram_got[p]
            outs[k][j, GRAM:] = cross[p] + cross_got[p]


def plane_second_kernel(at, a, b, c, d, *outs):
    for k in range(4):
        p = (at[1] + k) & 3
        outs[k][...] = (a[p] + b[p]) + (c[p] + d[p])


def line_first_kernel(at, *refs):
    ins, outs = refs[:4], refs[4:]
    rows = PART // 8
    for k in range(4):
        for h in range(2):
            start = (h * 4 + ((at[4] + k) & 3)) * rows
            lines = pl.ds(pl.multiple_of(start, 8), rows)
            a, b, c, d = (r[lines, :] for r in ins)
            outs[k][h] = (a + b) + (c + d)


def line_second_kernel(a, b, c, d, out):
    out[...] = (a[...] + b[...]) + (c[...] + d[...])


def line_third_kernel(a, b, out):
    out[...] = a[...] + b[...]


def gather_kernel(at, a, b, c, d, early, late, cross, piece):
    rows = PART // 8
    for k, got in enumerate((a, b, c, d)):
        for h in range(2):
            start = (h * 4 + ((at[4] - k) & 3)) * rows
            piece[pl.ds(pl.multiple_of(start, 8), rows), :] = got[h]
    for out, lo, hi in ((early, 0, EARLY_ROWS), (late, EARLY_ROWS, GRAM), (cross, GRAM, PART)):
        out[...] = jnp.broadcast_to(piece[lo:hi, :][None], out.shape)


def sum_of_chips(at, gram, gram_got, cross, cross_got):
    share = (2, PART // 8, NB)
    pieces = call(plane_first_kernel, [(4, PART, NB)] * 4, 1, 4)(at, gram, gram_got, cross, cross_got)
    pieces = call(plane_second_kernel, [(PART, NB)] * 4, 1, 4)(at, *along_plane(pieces, 0))
    pieces = call(line_first_kernel, [share] * 4, 1, 4)(at, *along_plane(pieces, 1))
    (mine,) = call(line_second_kernel, [share], 0, 4)(*along_line(pieces, "z_lo"))
    (mine,) = call(line_third_kernel, [share], 0, 2)(*along_line([mine] * 2, "z_hi"))
    wide = [(16, n, NB) for n in (EARLY_ROWS, GRAM - EARLY_ROWS, PART - GRAM)]
    return call(gather_kernel, wide, 1, 4, [pltpu.VMEM((PART, NB), jnp.float32)])(at, *along_line([mine] * 4, "z_lo"))


def tile(v):
    return jnp.broadcast_to(v, (G, NB))


def pivots(s):
    l = [[None] * G for _ in range(G)]
    r = [None] * G
    for k in range(G):
        r[k] = lax.rsqrt(s[k][k])
        for j in range(k + 1, G):
            l[j][k] = s[k][j] * r[k]
        for i in range(k + 1, G):
            for j in range(i, G):
                s[i][j] = s[i][j] - l[i][k] * l[j][k]
    return l, r


def forward(l, r, rows):
    out = []
    for k in range(G):
        v = rows[k]
        for j in range(k):
            v = v - l[k][j] * out[j]
        out.append(v * r[k])
    return out


def factor_block(work):
    groups = SB // G
    for top in range(0, NB, SB):
        left = [work[top + G * g:top + G * (g + 1), :NB] for g in range(groups)]
        right = [work[top + G * g:top + G * (g + 1), NB:] for g in range(groups)]
        for p in range(groups):
            c0 = top + G * p
            s = [[tile(left[p][i:i + 1, c0 + j:c0 + j + 1]) if j >= i else None for j in range(G)] for i in range(G)]
            cols = [
                [jnp.broadcast_to(left[q][:, c0 + k:c0 + k + 1], (G, NB)) for k in range(G)]
                for q in range(p + 1, groups)
            ]
            l, r = pivots(s)
            u = forward(l, r, [tile(left[p][i:i + 1, :]) for i in range(G)])
            b = forward(l, r, [tile(right[p][i:i + 1, :]) for i in range(G)])
            for i in range(G):
                work[c0 + i:c0 + i + 1, :NB] = u[i][0:1]
                work[c0 + i:c0 + i + 1, NB:] = b[i][0:1]
            for q in range(p + 1, groups):
                lc = forward(l, r, cols[q - p - 1])
                for k in range(G):
                    left[q] = left[q] - lc[k] * u[k]
                    right[q] = right[q] - lc[k] * b[k]
        rest = top + SB
        if rest < NB:
            rows = work[top:rest, :]
            work[rest:, :] -= mm(rows[:, rest:NB], rows, ((0,), (0,)))


def eliminate(first, last, width, upper, inverse, work):
    eye = lax.broadcasted_iota(jnp.int32, (NB, NB), 0) == lax.broadcasted_iota(jnp.int32, (NB, NB), 1)

    def step(k, carry):
        at = pl.multiple_of(k * NB, NB)
        work[:, :NB] = upper[pl.ds(at, NB), pl.ds(at, NB)]
        work[:, NB:] = eye.astype(jnp.float32)
        factor_block(work)
        inverse[pl.ds(at, NB), :] = work[:, NB:]
        for kk in range(first, min(last, width - 1)):
            @pl.when(k == kk)
            def _():
                lo, nxt, end = kk * NB, (kk + 1) * NB, width * NB
                upper[lo:nxt, nxt:end] = mm(work[:, NB:], upper[lo:nxt, nxt:end], ((1,), (0,)))
                for i in range(kk + 1, width):
                    rows = upper[lo:nxt, i * NB:end]
                    upper[i * NB:(i + 1) * NB, i * NB:end] -= mm(rows[:, :NB], rows, ((0,), (0,)))
        return carry

    lax.fori_loop(first, last, step, 0)


def head_kernel(blocks, upper, inverse, work):
    for at, (i, j) in enumerate(EARLY):
        upper[i * NB:(i + 1) * NB, j * NB:(j + 1) * NB] = blocks[at * NB:(at + 1) * NB, :]
    eliminate(0, HEAD, HEAD, upper, inverse, work)


def tail_kernel(rows, blocks, head, head_inverse, upper, inverse, z, work):
    h = HEAD * NB
    upper[:h, :h] = head[...]
    inverse[:h, :] = head_inverse[...]
    for at, (i, j) in enumerate(LATE):
        upper[i * NB:(i + 1) * NB, j * NB:(j + 1) * NB] = blocks[at * NB:(at + 1) * NB, :]
    for k in range(HEAD):
        lo, nxt = k * NB, (k + 1) * NB
        v = upper[lo:nxt, h:]
        if k:
            v = v - mm(upper[:lo, lo:nxt], upper[:lo, h:], ((0,), (0,)))
        upper[lo:nxt, h:] = mm(inverse[lo:nxt, :], v, ((1,), (0,)))
    for i in range(HEAD, KB):
        done = upper[:h, i * NB:]
        upper[i * NB:(i + 1) * NB, i * NB:] -= mm(done[:, :NB], done, ((0,), (0,)))
    eliminate(HEAD, KB, KB, upper, inverse, work)
    line = lax.broadcasted_iota(jnp.int32, (G, NB), 0)
    want = jnp.where(line < OWNED, rows[0] + line, rows[1] + line - OWNED)
    lane = lax.broadcasted_iota(jnp.int32, (G, NB), 1)
    for k in reversed(range(KB)):
        v = (want == lane + k * NB).astype(jnp.float32)
        if k < KB - 1:
            v = v - mm(z[:, (k + 1) * NB:], upper[k * NB:(k + 1) * NB, (k + 1) * NB:], ((1,), (1,)))
        z[:, k * NB:(k + 1) * NB] = mm(v, inverse[k * NB:(k + 1) * NB, :], ((1,), (0,)))


def apply_kernel(core, z_own, z_sent, cross, out):
    half = N // 2
    z = jnp.where(core[0] == 0, z_own[:, :half], z_sent[:, half:])
    acc = jnp.zeros((G, N), jnp.float32)
    for i in range(half // NB):
        row = jnp.concatenate([cross[(i * KB + j) // 2, j % 2 * NB:(j % 2 + 1) * NB, :] for j in range(KB)], axis=1)
        acc = acc + mm(z[:, i * NB:(i + 1) * NB], row, ((1,), (0,)))
    out[...] = acc


def solve_kernel(w_own, w_sent, upper, inverse, y):
    w = w_own[...] + w_sent[...]
    for k in range(KB):
        v = w[:, k * NB:(k + 1) * NB]
        if k:
            v = v - mm(y[:, :k * NB], upper[:k * NB, k * NB:(k + 1) * NB], ((1,), (0,)))
        y[:, k * NB:(k + 1) * NB] = mm(v, inverse[k * NB:(k + 1) * NB, :], ((1,), (1,)))


def after(value, *others):
    return lax.optimization_barrier((value, *others))[0]


def on_device(view_x, view_y):
    core = lax.axis_index("core")
    core_ref = core.astype(jnp.int32).reshape(1)
    x, y, z_lo, z_hi = (lax.axis_index(a).astype(jnp.int32) for a in ("x", "y", "z_lo", "z_hi"))
    at = jnp.stack([*jnp.where(core == 0, jnp.array([x, y, 4, 1]), jnp.array([y, x, 1, 4])), z_lo]).astype(jnp.int32)
    chip = (z_hi * 4 + x) * 32 + y * 4 + z_lo
    rows = jnp.stack([chip * OWNED, (chip + 16) * OWNED])
    work = pltpu.VMEM((NB, 2 * NB), jnp.float32)

    with jax.named_scope("sums"):
        gram, gram_other = call(
            gram_kernel, [(16, GRAM, NB)] * 2, 1, 2, [pltpu.VMEM(view_x.shape, view_x.dtype)], flops=2 * 10**9
        )(core_ref, view_x, view_y)
        cross, cross_other = call(cross_kernel, [(16, PART - GRAM, NB)] * 2, 1, 2, flops=10**9)(
            core_ref, *after((view_x, view_y), gram)
        )
        early, late, cross = sum_of_chips(at, gram, swap(gram_other), cross, swap(cross_other))
    with jax.named_scope("back"):
        early = exchange(early, PLANE)
        late = exchange(after(late, early), PLANE)
        cross = exchange(after(cross, late), PLANE)
        early, late = early.reshape(-1, NB), late.reshape(-1, NB)

    head, head_inverse = call(
        head_kernel, [(HEAD * NB, HEAD * NB), (HEAD * NB, NB)], 0, 1, [work], flops=3 * 10**10
    )(early)
    upper, inverse, z = call(tail_kernel, [(N, N), (N, NB), (G, N)], 1, 3, [work], flops=4 * 10**10)(
        rows, late, head, head_inverse
    )
    (w,) = call(apply_kernel, [(G, N)], 1, 3)(core_ref, z, swap(z), cross)
    (y_rows,) = call(solve_kernel, [(G, N)], 0, 4)(w, swap(w), upper, inverse)
    y_sent = swap(y_rows[:OWNED])
    return jnp.where(core == 0, y_sent, y_rows[OWNED:])


def solution(mesh):
    fine = Mesh(mesh.devices.reshape(SIZES), AXES)
    spec = P(AXES, None)
    return jax.shard_map(on_device, mesh=fine, in_specs=(spec, spec), out_specs=spec, check_vma=False)
```

```python
import functools

import jax
import jax.numpy as jnp
from jax import lax
from jax.experimental import pallas as pl
from jax.experimental.pallas import tpu as pltpu
from jax.sharding import Mesh
from jax.sharding import PartitionSpec as P

AXES = ("z_hi", "x", "core", "y", "z_lo")
SIZES = (2, 4, 2, 4, 4)
PLANE = ("x", "y")
N, NB, SB, G = 1024, 128, 64, 8
KB = N // NB
OWNED = 4
HEAD = 5
EARLY = [(i, j) for i in range(HEAD) for j in range(i, HEAD)]
LATE = [(i, j) for i in range(KB) for j in range(max(i, HEAD), KB)]
LATE_SLOTS = 40 - len(EARLY)
STEP = 8
EARLY_ROWS = len(EARLY) * NB // 16
GRAM = 40 * NB // 16
PART = GRAM + N // 2 * N // NB // 16
VMEM = pl.BlockSpec(memory_space=pltpu.VMEM)
SMEM = pl.BlockSpec(memory_space=pltpu.SMEM)
HBM = pl.BlockSpec(memory_space=pltpu.HBM)


def mm(a, b, dims):
    return lax.dot_general(
        a, b, (dims, ((), ())), precision=lax.Precision.HIGHEST, preferred_element_type=jnp.float32
    )


def call(kernel, outs, n_smem, n_vmem, scratch=(), flops=0, n_hbm=0, hbm_outs=0):
    return pl.pallas_call(
        kernel,
        out_shape=[jax.ShapeDtypeStruct(s, jnp.float32) for s in outs],
        in_specs=[SMEM] * n_smem + [HBM] * n_hbm + [VMEM] * n_vmem,
        out_specs=[HBM] * hbm_outs + [VMEM] * (len(outs) - hbm_outs),
        scratch_shapes=list(scratch),
        compiler_params=pltpu.CompilerParams(vmem_limit_bytes=(60 if n_hbm + hbm_outs else 16) << 20),
        cost_estimate=pl.CostEstimate(flops=flops, bytes_accessed=0, transcendentals=0),
    )


def gram_kernel(core, x, y, mine, other, pick):
    early_rows, late_rows = EARLY_ROWS, GRAM - EARLY_ROWS
    for out, which in ((mine, 0), (other, 1)):
        @pl.when(core[0] == which)
        def _():
            pick[...] = x[...]

        @pl.when(core[0] != which)
        def _():
            pick[...] = y[...]

        for i in range(KB):
            prod = lax.dot_general(
                pick[:, i * NB:(i + 1) * NB], pick[:, i * NB:], (((0,), (0,)), ((), ())),
                preferred_element_type=jnp.float32,
            )
            for j in range(i, KB):
                early = (i, j) in EARLY
                at = (EARLY if early else LATE).index((i, j)) * NB
                rows, base = (early_rows, 0) if early else (late_rows, early_rows)
                for t in range(0, NB, STEP):
                    part, line = divmod(at + t, rows)
                    out[part, base + line:base + line + STEP, :] = prod[t:t + STEP, (j - i) * NB:(j - i + 1) * NB]
        for at in range(len(LATE) * NB, LATE_SLOTS * NB, STEP):
            part, line = divmod(at, late_rows)
            out[part, early_rows + line:early_rows + line + STEP, :] = jnp.zeros((STEP, NB), jnp.float32)


def cross_kernel(core, x, y, mine, other):
    half = N // 2
    for out, which in ((mine, core[0]), (other, 1 - core[0])):
        left = x[:, pl.ds(pl.multiple_of(which * half, half), half)]
        for j in range(KB // 2):
            prod = lax.dot_general(
                left, y[:, 2 * j * NB:2 * (j + 1) * NB], (((0,), (0,)), ((), ())), preferred_element_type=jnp.float32
            )
            for i in range(half // NB):
                for d in range(2):
                    out[i * KB // 2 + j, d * NB:(d + 1) * NB, :] = prod[i * NB:(i + 1) * NB, d * NB:(d + 1) * NB]


def exchange(pieces, axes):
    return lax.all_to_all(pieces, axes, 0, 0, tiled=True)


def swap(a):
    return lax.ppermute(a, "core", [(0, 1), (1, 0)])


def plane_route(k, step):
    return [
        ((x * 2 + c) * 4 + y, ((x + k) % 4 * 2 + c) * 4 + y if c == step else (x * 2 + c) * 4 + (y + k) % 4)
        for x in range(4) for c in range(2) for y in range(4)
    ]


def shift(pieces, axes, route):
    return [lax.ppermute(p, axes, route(k)) if k else p for k, p in enumerate(pieces)]


def along_plane(pieces, step):
    return shift(pieces, ("x", "core", "y"), lambda k: plane_route(k, step))


def along_line(pieces, axis):
    size = len(pieces)
    return shift(pieces, axis, lambda k: [(i, (i + k) % size) for i in range(size)])


def plane_first_kernel(at, gram, gram_got, cross, cross_got, *outs):
    for k in range(4):
        for j in range(4):
            p = ((at[0] + k) & 3) * at[2] + j * at[3]
            outs[k][j, :GRAM] = gram[p] + gram_got[p]
            outs[k][j, GRAM:] = cross[p] + cross_got[p]


def plane_second_kernel(at, a, b, c, d, *outs):
    for k in range(4):
        p = (at[1] + k) & 3
        outs[k][...] = (a[p] + b[p]) + (c[p] + d[p])


def line_first_kernel(at, *refs):
    ins, outs = refs[:4], refs[4:]
    rows = PART // 8
    for k in range(4):
        for h in range(2):
            start = (h * 4 + ((at[4] + k) & 3)) * rows
            lines = pl.ds(pl.multiple_of(start, 8), rows)
            a, b, c, d = (r[lines, :] for r in ins)
            outs[k][h] = (a + b) + (c + d)


def line_second_kernel(a, b, c, d, out):
    out[...] = (a[...] + b[...]) + (c[...] + d[...])


def line_third_kernel(a, b, out):
    out[...] = a[...] + b[...]


def gather_kernel(at, a, b, c, d, early, late, cross, piece):
    rows = PART // 8
    for k, got in enumerate((a, b, c, d)):
        for h in range(2):
            start = (h * 4 + ((at[4] - k) & 3)) * rows
            piece[pl.ds(pl.multiple_of(start, 8), rows), :] = got[h]
    for out, lo, hi in ((early, 0, EARLY_ROWS), (late, EARLY_ROWS, GRAM), (cross, GRAM, PART)):
        out[...] = jnp.broadcast_to(piece[lo:hi, :][None], out.shape)


def sum_of_chips(at, gram, gram_got, cross, cross_got):
    share = (2, PART // 8, NB)
    pieces = call(plane_first_kernel, [(4, PART, NB)] * 4, 1, 4)(at, gram, gram_got, cross, cross_got)
    pieces = call(plane_second_kernel, [(PART, NB)] * 4, 1, 4)(at, *along_plane(pieces, 0))
    pieces = call(line_first_kernel, [share] * 4, 1, 4)(at, *along_plane(pieces, 1))
    (mine,) = call(line_second_kernel, [share], 0, 4)(*along_line(pieces, "z_lo"))
    (mine,) = call(line_third_kernel, [share], 0, 2)(*along_line([mine] * 2, "z_hi"))
    wide = [(16, n, NB) for n in (EARLY_ROWS, GRAM - EARLY_ROWS, PART - GRAM)]
    return call(gather_kernel, wide, 1, 4, [pltpu.VMEM((PART, NB), jnp.float32)])(at, *along_line([mine] * 4, "z_lo"))


def tile(v):
    return jnp.broadcast_to(v, (G, NB))


def pivots(s):
    l = [[None] * G for _ in range(G)]
    r = [None] * G
    for k in range(G):
        r[k] = lax.rsqrt(s[k][k])
        for j in range(k + 1, G):
            l[j][k] = s[k][j] * r[k]
        for i in range(k + 1, G):
            for j in range(i, G):
                s[i][j] = s[i][j] - l[i][k] * l[j][k]
    return l, r


def forward(l, r, rows):
    out = []
    for k in range(G):
        v = rows[k]
        for j in range(k):
            v = v - l[k][j] * out[j]
        out.append(v * r[k])
    return out


def factor_block(work):
    groups = SB // G
    for top in range(0, NB, SB):
        left = [work[top + G * g:top + G * (g + 1), :NB] for g in range(groups)]
        right = [work[top + G * g:top + G * (g + 1), NB:] for g in range(groups)]
        for p in range(groups):
            c0 = top + G * p
            s = [[tile(left[p][i:i + 1, c0 + j:c0 + j + 1]) if j >= i else None for j in range(G)] for i in range(G)]
            cols = [
                [jnp.broadcast_to(left[q][:, c0 + k:c0 + k + 1], (G, NB)) for k in range(G)]
                for q in range(p + 1, groups)
            ]
            l, r = pivots(s)
            u = forward(l, r, [tile(left[p][i:i + 1, :]) for i in range(G)])
            b = forward(l, r, [tile(right[p][i:i + 1, :]) for i in range(G)])
            for i in range(G):
                work[c0 + i:c0 + i + 1, :NB] = u[i][0:1]
                work[c0 + i:c0 + i + 1, NB:] = b[i][0:1]
            for q in range(p + 1, groups):
                lc = forward(l, r, cols[q - p - 1])
                for k in range(G):
                    left[q] = left[q] - lc[k] * u[k]
                    right[q] = right[q] - lc[k] * b[k]
        rest = top + SB
        if rest < NB:
            rows = work[top:rest, :]
            work[rest:, :] -= mm(rows[:, rest:NB], rows, ((0,), (0,)))


def eliminate(first, last, width, upper, inverse, work):
    eye = lax.broadcasted_iota(jnp.int32, (NB, NB), 0) == lax.broadcasted_iota(jnp.int32, (NB, NB), 1)

    def step(k, carry):
        at = pl.multiple_of(k * NB, NB)
        work[:, :NB] = upper[pl.ds(at, NB), pl.ds(at, NB)]
        work[:, NB:] = eye.astype(jnp.float32)
        factor_block(work)
        inverse[pl.ds(at, NB), :] = work[:, NB:]
        for kk in range(first, min(last, width - 1)):
            @pl.when(k == kk)
            def _():
                lo, nxt, end = kk * NB, (kk + 1) * NB, width * NB
                upper[lo:nxt, nxt:end] = mm(work[:, NB:], upper[lo:nxt, nxt:end], ((1,), (0,)))
                for i in range(kk + 1, width):
                    rows = upper[lo:nxt, i * NB:end]
                    upper[i * NB:(i + 1) * NB, i * NB:end] -= mm(rows[:, :NB], rows, ((0,), (0,)))
        return carry

    lax.fori_loop(first, last, step, 0)


def right_of(ref, i, end):
    return ref.at[pl.ds(i * NB, NB), pl.ds((i + 1) * NB, end - (i + 1) * NB)]


def block(ref, i, j):
    return ref.at[pl.ds(i * NB, NB), pl.ds(j * NB, NB)]


def head_kernel(blocks, head, inverse, upper, work, sems):
    for at, (i, j) in enumerate(EARLY):
        upper[i * NB:(i + 1) * NB, j * NB:(j + 1) * NB] = blocks[at * NB:(at + 1) * NB, :]
    eliminate(0, HEAD, HEAD, upper, inverse, work)
    copies = [
        pltpu.make_async_copy(right_of(upper, i, HEAD * NB), right_of(head, i, HEAD * NB), sems.at[i])
        for i in range(HEAD - 1)
    ]
    for c in copies:
        c.start()
    for c in copies:
        c.wait()


def tail_kernel(rows, late, head, head_inverse, factor, inverse, z, upper, work, in_sems, out_sems):
    h = HEAD * NB
    copies = [
        pltpu.make_async_copy(late.at[pl.ds(at * NB, NB), :], block(upper, i, j), in_sems.at[at])
        for at, (i, j) in enumerate(LATE)
    ] + [
        pltpu.make_async_copy(right_of(head, i, h), right_of(upper, i, h), in_sems.at[len(LATE) + i])
        for i in range(HEAD - 1)
    ]
    for c in copies:
        c.start()
    inverse[:h, :] = head_inverse[...]
    for c in copies:
        c.wait()
    for k in range(HEAD):
        lo, nxt = k * NB, (k + 1) * NB
        v = upper[lo:nxt, h:]
        if k:
            v = v - mm(upper[:lo, lo:nxt], upper[:lo, h:], ((0,), (0,)))
        upper[lo:nxt, h:] = mm(inverse[lo:nxt, :], v, ((1,), (0,)))
    for i in range(HEAD, KB):
        done = upper[:h, i * NB:]
        upper[i * NB:(i + 1) * NB, i * NB:] -= mm(done[:, :NB], done, ((0,), (0,)))
    copies = [
        pltpu.make_async_copy(right_of(upper, i, N), right_of(factor, i, N), out_sems.at[i]) for i in range(KB - 1)
    ]
    for c in copies[:HEAD]:
        c.start()
    eliminate(HEAD, KB, KB, upper, inverse, work)
    for c in copies[HEAD:]:
        c.start()
    line = lax.broadcasted_iota(jnp.int32, (G, NB), 0)
    want = jnp.where(line < OWNED, rows[0] + line, rows[1] + line - OWNED)
    lane = lax.broadcasted_iota(jnp.int32, (G, NB), 1)
    for k in reversed(range(KB)):
        v = (want == lane + k * NB).astype(jnp.float32)
        if k < KB - 1:
            v = v - mm(z[:, (k + 1) * NB:], upper[k * NB:(k + 1) * NB, (k + 1) * NB:], ((1,), (1,)))
        z[:, k * NB:(k + 1) * NB] = mm(v, inverse[k * NB:(k + 1) * NB, :], ((1,), (0,)))
    for c in copies:
        c.wait()


def apply_kernel(core, z_own, z_sent, cross, out):
    half = N // 2
    z = jnp.where(core[0] == 0, z_own[:, :half], z_sent[:, half:])
    acc = jnp.zeros((G, N), jnp.float32)
    for i in range(half // NB):
        row = jnp.concatenate([cross[(i * KB + j) // 2, j % 2 * NB:(j % 2 + 1) * NB, :] for j in range(KB)], axis=1)
        acc = acc + mm(z[:, i * NB:(i + 1) * NB], row, ((1,), (0,)))
    out[...] = acc


def solve_kernel(factor, w_own, w_sent, inverse, y, upper, sems):
    copies = [
        pltpu.make_async_copy(
            factor.at[pl.ds(0, k * NB), pl.ds(k * NB, NB)], upper.at[pl.ds(0, k * NB), pl.ds(k * NB, NB)], sems.at[k - 1]
        )
        for k in range(1, KB)
    ]
    for c in copies:
        c.start()
    w = w_own[...] + w_sent[...]
    for k in range(KB):
        v = w[:, k * NB:(k + 1) * NB]
        if k:
            copies[k - 1].wait()
            v = v - mm(y[:, :k * NB], upper[:k * NB, k * NB:(k + 1) * NB], ((1,), (0,)))
        y[:, k * NB:(k + 1) * NB] = mm(v, inverse[k * NB:(k + 1) * NB, :], ((1,), (1,)))


def after(value, *others):
    return lax.optimization_barrier((value, *others))[0]


def on_device(view_x, view_y):
    core = lax.axis_index("core")
    core_ref = core.astype(jnp.int32).reshape(1)
    x, y, z_lo, z_hi = (lax.axis_index(a).astype(jnp.int32) for a in ("x", "y", "z_lo", "z_hi"))
    at = jnp.stack([*jnp.where(core == 0, jnp.array([x, y, 4, 1]), jnp.array([y, x, 1, 4])), z_lo]).astype(jnp.int32)
    chip = (z_hi * 4 + x) * 32 + y * 4 + z_lo
    rows = jnp.stack([chip * OWNED, (chip + 16) * OWNED])
    work = pltpu.VMEM((NB, 2 * NB), jnp.float32)

    with jax.named_scope("sums"):
        gram, gram_other = call(
            gram_kernel, [(16, GRAM, NB)] * 2, 1, 2, [pltpu.VMEM(view_x.shape, view_x.dtype)], flops=2 * 10**9
        )(core_ref, view_x, view_y)
        cross, cross_other = call(cross_kernel, [(16, PART - GRAM, NB)] * 2, 1, 2, flops=10**9)(
            core_ref, *after((view_x, view_y), gram)
        )
        early, late, cross = sum_of_chips(at, gram, swap(gram_other), cross, swap(cross_other))
    with jax.named_scope("back"):
        early = exchange(early, PLANE)
        late = exchange(after(late, early), PLANE)
        cross = exchange(after(cross, late), PLANE)
        early, late = early.reshape(-1, NB), late.reshape(-1, NB)

    size = HEAD * NB
    dma = pltpu.SemaphoreType.DMA
    square = pltpu.VMEM((N, N), jnp.float32)
    head, head_inverse = call(
        head_kernel, [(size, size), (size, NB)], 0, 1,
        [pltpu.VMEM((size, size), jnp.float32), work, dma((HEAD - 1,))], flops=3 * 10**10, hbm_outs=1,
    )(early)
    factor, inverse, z = call(
        tail_kernel, [(N, N), (N, NB), (G, N)], 1, 1,
        [square, work, dma((len(LATE) + HEAD - 1,)), dma((KB - 1,))], flops=4 * 10**10, n_hbm=2, hbm_outs=1,
    )(rows, late, head, head_inverse)
    (w,) = call(apply_kernel, [(G, N)], 1, 3)(core_ref, z, swap(z), cross)
    (y_rows,) = call(solve_kernel, [(G, N)], 0, 3, [square, dma((KB - 1,))], n_hbm=1)(factor, w, swap(w), inverse)
    y_sent = swap(y_rows[:OWNED])
    return jnp.where(core == 0, y_sent, y_rows[OWNED:])


def solution(mesh):
    fine = Mesh(mesh.devices.reshape(SIZES), AXES)
    spec = P(AXES, None)
    return jax.shard_map(on_device, mesh=fine, in_specs=(spec, spec), out_specs=spec, check_vma=False)
```

```python
import functools

import jax
import jax.numpy as jnp
from jax import lax
from jax.experimental import pallas as pl
from jax.experimental.pallas import tpu as pltpu
from jax.sharding import Mesh
from jax.sharding import PartitionSpec as P

AXES = ("z_hi", "x", "core", "y", "z_lo")
SIZES = (2, 4, 2, 4, 4)
PLANE = ("x", "y")
N, NB, SB, G = 1024, 128, 64, 8
KB = N // NB
OWNED = 4
HEAD = 5
EARLY = [(i, j) for i in range(HEAD) for j in range(i, HEAD)]
LATE = [(i, j) for i in range(KB) for j in range(max(i, HEAD), KB)]
LATE_SLOTS = 40 - len(EARLY)
STEP = 8
EARLY_ROWS = len(EARLY) * NB // 16
GRAM = 40 * NB // 16
PART = GRAM + N // 2 * N // NB // 16
VMEM = pl.BlockSpec(memory_space=pltpu.VMEM)
SMEM = pl.BlockSpec(memory_space=pltpu.SMEM)


def mm(a, b, dims):
    return lax.dot_general(
        a, b, (dims, ((), ())), precision=lax.Precision.HIGHEST, preferred_element_type=jnp.float32
    )


def call(kernel, outs, n_smem, n_vmem, scratch=(), flops=0, bytes_accessed=0):
    return pl.pallas_call(
        kernel,
        out_shape=[jax.ShapeDtypeStruct(s, jnp.float32) for s in outs],
        in_specs=[SMEM] * n_smem + [VMEM] * n_vmem,
        out_specs=[VMEM] * len(outs),
        scratch_shapes=list(scratch),
        compiler_params=pltpu.CompilerParams(vmem_limit_bytes=16 << 20),
        cost_estimate=pl.CostEstimate(flops=flops, bytes_accessed=bytes_accessed, transcendentals=0),
    )


def gram_kernel(core, x, y, mine, other, pick):
    early_rows, late_rows = EARLY_ROWS, GRAM - EARLY_ROWS
    for out, which in ((mine, 0), (other, 1)):
        @pl.when(core[0] == which)
        def _():
            pick[...] = x[...]

        @pl.when(core[0] != which)
        def _():
            pick[...] = y[...]

        for i in range(KB):
            prod = lax.dot_general(
                pick[:, i * NB:(i + 1) * NB], pick[:, i * NB:], (((0,), (0,)), ((), ())),
                preferred_element_type=jnp.float32,
            )
            for j in range(i, KB):
                early = (i, j) in EARLY
                at = (EARLY if early else LATE).index((i, j)) * NB
                rows, base = (early_rows, 0) if early else (late_rows, early_rows)
                for t in range(0, NB, STEP):
                    part, line = divmod(at + t, rows)
                    out[part, base + line:base + line + STEP, :] = prod[t:t + STEP, (j - i) * NB:(j - i + 1) * NB]
        for at in range(len(LATE) * NB, LATE_SLOTS * NB, STEP):
            part, line = divmod(at, late_rows)
            out[part, early_rows + line:early_rows + line + STEP, :] = jnp.zeros((STEP, NB), jnp.float32)


def cross_kernel(core, x, y, mine, other):
    half = N // 2
    for out, which in ((mine, core[0]), (other, 1 - core[0])):
        left = x[:, pl.ds(pl.multiple_of(which * half, half), half)]
        for j in range(KB // 2):
            prod = lax.dot_general(
                left, y[:, 2 * j * NB:2 * (j + 1) * NB], (((0,), (0,)), ((), ())), preferred_element_type=jnp.float32
            )
            for i in range(half // NB):
                for d in range(2):
                    out[i * KB // 2 + j, d * NB:(d + 1) * NB, :] = prod[i * NB:(i + 1) * NB, d * NB:(d + 1) * NB]


def exchange(pieces, axes):
    return lax.all_to_all(pieces, axes, 0, 0, tiled=True)


def swap(a):
    return lax.ppermute(a, "core", [(0, 1), (1, 0)])


def plane_route(k, step):
    return [
        ((x * 2 + c) * 4 + y, ((x + k) % 4 * 2 + c) * 4 + y if c == step else (x * 2 + c) * 4 + (y + k) % 4)
        for x in range(4) for c in range(2) for y in range(4)
    ]


def shift(pieces, axes, route):
    return [lax.ppermute(p, axes, route(k)) if k else p for k, p in enumerate(pieces)]


def along_plane(pieces, step):
    return shift(pieces, ("x", "core", "y"), lambda k: plane_route(k, step))


def along_line(pieces, axis):
    size = len(pieces)
    return shift(pieces, axis, lambda k: [(i, (i + k) % size) for i in range(size)])


def plane_first_kernel(at, gram, gram_got, cross, cross_got, *outs):
    for k in range(4):
        for j in range(4):
            p = ((at[0] + k) & 3) * at[2] + j * at[3]
            outs[k][j, :GRAM] = gram[p] + gram_got[p]
            outs[k][j, GRAM:] = cross[p] + cross_got[p]


def plane_second_kernel(at, a, b, c, d, *outs):
    for k in range(4):
        p = (at[1] + k) & 3
        outs[k][...] = (a[p] + b[p]) + (c[p] + d[p])


def line_first_kernel(at, *refs):
    ins, outs = refs[:4], refs[4:]
    rows = PART // 8
    for k in range(4):
        for h in range(2):
            start = (h * 4 + ((at[4] + k) & 3)) * rows
            lines = pl.ds(pl.multiple_of(start, 8), rows)
            a, b, c, d = (r[lines, :] for r in ins)
            outs[k][h] = (a + b) + (c + d)


def line_second_kernel(a, b, c, d, out):
    out[...] = (a[...] + b[...]) + (c[...] + d[...])


def line_third_kernel(a, b, out):
    out[...] = a[...] + b[...]


def gather_kernel(at, a, b, c, d, early, late, cross, piece):
    rows = PART // 8
    for k, got in enumerate((a, b, c, d)):
        for h in range(2):
            start = (h * 4 + ((at[4] - k) & 3)) * rows
            piece[pl.ds(pl.multiple_of(start, 8), rows), :] = got[h]
    for out, lo, hi in ((early, 0, EARLY_ROWS), (late, EARLY_ROWS, GRAM), (cross, GRAM, PART)):
        out[...] = jnp.broadcast_to(piece[lo:hi, :][None], out.shape)


def sum_of_chips(at, gram, gram_got, cross, cross_got):
    share = (2, PART // 8, NB)
    pieces = call(plane_first_kernel, [(4, PART, NB)] * 4, 1, 4)(at, gram, gram_got, cross, cross_got)
    pieces = call(plane_second_kernel, [(PART, NB)] * 4, 1, 4)(at, *along_plane(pieces, 0))
    pieces = call(line_first_kernel, [share] * 4, 1, 4)(at, *along_plane(pieces, 1))
    (mine,) = call(line_second_kernel, [share], 0, 4)(*along_line(pieces, "z_lo"))
    (mine,) = call(line_third_kernel, [share], 0, 2)(*along_line([mine] * 2, "z_hi"))
    wide = [(16, n, NB) for n in (EARLY_ROWS, GRAM - EARLY_ROWS, PART - GRAM)]
    return call(gather_kernel, wide, 1, 4, [pltpu.VMEM((PART, NB), jnp.float32)])(at, *along_line([mine] * 4, "z_lo"))


def tile(v):
    return jnp.broadcast_to(v, (G, NB))


def pivots(s):
    l = [[None] * G for _ in range(G)]
    r = [None] * G
    for k in range(G):
        r[k] = lax.rsqrt(s[k][k])
        for j in range(k + 1, G):
            l[j][k] = s[k][j] * r[k]
        for i in range(k + 1, G):
            for j in range(i, G):
                s[i][j] = s[i][j] - l[i][k] * l[j][k]
    return l, r


def forward(l, r, rows):
    out = []
    for k in range(G):
        v = rows[k]
        for j in range(k):
            v = v - l[k][j] * out[j]
        out.append(v * r[k])
    return out


def factor_block(work):
    groups = SB // G
    for top in range(0, NB, SB):
        left = [work[top + G * g:top + G * (g + 1), :NB] for g in range(groups)]
        right = [work[top + G * g:top + G * (g + 1), NB:] for g in range(groups)]
        for p in range(groups):
            c0 = top + G * p
            s = [[tile(left[p][i:i + 1, c0 + j:c0 + j + 1]) if j >= i else None for j in range(G)] for i in range(G)]
            cols = [
                [jnp.broadcast_to(left[q][:, c0 + k:c0 + k + 1], (G, NB)) for k in range(G)]
                for q in range(p + 1, groups)
            ]
            l, r = pivots(s)
            u = forward(l, r, [tile(left[p][i:i + 1, :]) for i in range(G)])
            b = forward(l, r, [tile(right[p][i:i + 1, :]) for i in range(G)])
            for i in range(G):
                work[c0 + i:c0 + i + 1, :NB] = u[i][0:1]
                work[c0 + i:c0 + i + 1, NB:] = b[i][0:1]
            for q in range(p + 1, groups):
                lc = forward(l, r, cols[q - p - 1])
                for k in range(G):
                    left[q] = left[q] - lc[k] * u[k]
                    right[q] = right[q] - lc[k] * b[k]
        rest = top + SB
        if rest < NB:
            rows = work[top:rest, :]
            work[rest:, :] -= mm(rows[:, rest:NB], rows, ((0,), (0,)))


def eliminate(first, last, width, upper, inverse, work):
    eye = lax.broadcasted_iota(jnp.int32, (NB, NB), 0) == lax.broadcasted_iota(jnp.int32, (NB, NB), 1)

    for k in range(first, last):
        lo, nxt, end = k * NB, (k + 1) * NB, width * NB
        work[:, :NB] = upper[lo:nxt, lo:nxt]
        work[:, NB:] = eye.astype(jnp.float32)
        factor_block(work)
        inverse[lo:nxt, :] = work[:, NB:]
        if k == width - 1:
            break
        upper[lo:nxt, nxt:end] = mm(work[:, NB:], upper[lo:nxt, nxt:end], ((1,), (0,)))
        for i in range(k + 1, width):
            rows = upper[lo:nxt, i * NB:end]
            upper[i * NB:(i + 1) * NB, i * NB:end] -= mm(rows[:, :NB], rows, ((0,), (0,)))


def head_kernel(blocks, upper, inverse, work):
    for at, (i, j) in enumerate(EARLY):
        upper[i * NB:(i + 1) * NB, j * NB:(j + 1) * NB] = blocks[at * NB:(at + 1) * NB, :]
    eliminate(0, HEAD, HEAD, upper, inverse, work)


def tail_kernel(rows, blocks, head, head_inverse, upper, inverse, z, work):
    h = HEAD * NB
    upper[:h, :h] = head[...]
    inverse[:h, :] = head_inverse[...]
    for at, (i, j) in enumerate(LATE):
        upper[i * NB:(i + 1) * NB, j * NB:(j + 1) * NB] = blocks[at * NB:(at + 1) * NB, :]
    for k in range(HEAD):
        lo, nxt = k * NB, (k + 1) * NB
        v = upper[lo:nxt, h:]
        if k:
            v = v - mm(upper[:lo, lo:nxt], upper[:lo, h:], ((0,), (0,)))
        upper[lo:nxt, h:] = mm(inverse[lo:nxt, :], v, ((1,), (0,)))
    for i in range(HEAD, KB):
        done = upper[:h, i * NB:]
        upper[i * NB:(i + 1) * NB, i * NB:] -= mm(done[:, :NB], done, ((0,), (0,)))
    eliminate(HEAD, KB, KB, upper, inverse, work)
    line = lax.broadcasted_iota(jnp.int32, (G, NB), 0)
    want = jnp.where(line < OWNED, rows[0] + line, rows[1] + line - OWNED)
    lane = lax.broadcasted_iota(jnp.int32, (G, NB), 1)
    for k in reversed(range(KB)):
        v = (want == lane + k * NB).astype(jnp.float32)
        if k < KB - 1:
            v = v - mm(z[:, (k + 1) * NB:], upper[k * NB:(k + 1) * NB, (k + 1) * NB:], ((1,), (1,)))
        z[:, k * NB:(k + 1) * NB] = mm(v, inverse[k * NB:(k + 1) * NB, :], ((1,), (0,)))


def apply_kernel(core, z_own, z_sent, cross, out):
    half = N // 2
    z = jnp.where(core[0] == 0, z_own[:, :half], z_sent[:, half:])
    acc = jnp.zeros((G, N), jnp.float32)
    for i in range(half // NB):
        row = jnp.concatenate([cross[(i * KB + j) // 2, j % 2 * NB:(j % 2 + 1) * NB, :] for j in range(KB)], axis=1)
        acc = acc + mm(z[:, i * NB:(i + 1) * NB], row, ((1,), (0,)))
    out[...] = acc


def solve_kernel(w_own, w_sent, upper, inverse, y):
    w = w_own[...] + w_sent[...]
    for k in range(KB):
        v = w[:, k * NB:(k + 1) * NB]
        if k:
            v = v - mm(y[:, :k * NB], upper[:k * NB, k * NB:(k + 1) * NB], ((1,), (0,)))
        y[:, k * NB:(k + 1) * NB] = mm(v, inverse[k * NB:(k + 1) * NB, :], ((1,), (1,)))


def after(value, *others):
    return lax.optimization_barrier((value, *others))[0]


def on_device(view_x, view_y):
    core = lax.axis_index("core")
    core_ref = core.astype(jnp.int32).reshape(1)
    x, y, z_lo, z_hi = (lax.axis_index(a).astype(jnp.int32) for a in ("x", "y", "z_lo", "z_hi"))
    at = jnp.stack([*jnp.where(core == 0, jnp.array([x, y, 4, 1]), jnp.array([y, x, 1, 4])), z_lo]).astype(jnp.int32)
    chip = (z_hi * 4 + x) * 32 + y * 4 + z_lo
    rows = jnp.stack([chip * OWNED, (chip + 16) * OWNED])
    work = pltpu.VMEM((NB, 2 * NB), jnp.float32)

    with jax.named_scope("sums"):
        gram, gram_other = call(
            gram_kernel, [(16, GRAM, NB)] * 2, 1, 2, [pltpu.VMEM(view_x.shape, view_x.dtype)], flops=2 * 10**9
        )(core_ref, view_x, view_y)
        cross, cross_other = call(cross_kernel, [(16, PART - GRAM, NB)] * 2, 1, 2, flops=10**9)(
            core_ref, *after((view_x, view_y), gram)
        )
        early, late, cross = sum_of_chips(at, gram, swap(gram_other), cross, swap(cross_other))
    with jax.named_scope("back"):
        early = exchange(early, PLANE)
        late = exchange(after(late, early), PLANE)
        cross = exchange(after(cross, late), PLANE)
        early, late = early.reshape(-1, NB), late.reshape(-1, NB)

    head, head_inverse = call(
        head_kernel, [(HEAD * NB, HEAD * NB), (HEAD * NB, NB)], 0, 1, [work], flops=3 * 10**10
    )(early)
    upper, inverse, z = call(tail_kernel, [(N, N), (N, NB), (G, N)], 1, 3, [work], flops=4 * 10**10)(
        rows, late, head, head_inverse
    )
    (w,) = call(apply_kernel, [(G, N)], 1, 3)(core_ref, z, swap(z), cross)
    (y_rows,) = call(solve_kernel, [(G, N)], 0, 4)(w, swap(w), upper, inverse)
    y_sent = swap(y_rows[:OWNED])
    return jnp.where(core == 0, y_sent, y_rows[OWNED:])


def solution(mesh):
    fine = Mesh(mesh.devices.reshape(SIZES), AXES)
    spec = P(AXES, None)
    return jax.shard_map(on_device, mesh=fine, in_specs=(spec, spec), out_specs=spec, check_vma=False)
```
